32 devices in a mesh: groups: 2 (over y), context: 4 (over z), tensor: 4 (over x, core).
Axes of the slice: x: 2, y: 2, z: 4, core: 2. Of those that a mesh axis runs over, the one named last changes fastest.
Arguments:
- hidden: bfloat16 [4096, 4096], P(('groups', 'context'), 'tensor'), parts along dimension 0, may hold values from -6 to 6
- norm_gain: float32 [4096], replicated, may hold values from 0.1 to 1.9
- in_proj: bfloat16 [4096, 3, 2048], P(None, None, 'tensor'), may hold values from -0.09375 to 0.09375
- short_filter: float32 [7, 3, 2048], P(None, None, 'tensor'), may hold values from -2 to 2
- conv_cache: bfloat16 [12, 3, 2048], P('groups', None, 'tensor'), parts along dimension 0, may hold values from -6 to 6
- decay: float32 [2048, 16], P('tensor'), may hold values from 9.765625e-06 to 0.05
- residues: float32 [2048, 16], P('tensor'), may hold values from -4 to 4
- skip_gain: float32 [2048], P('tensor'), may hold values from -6 to 6
- cached_state: float32 [4096, 16], P(('groups', 'tensor')), parts along dimension 0, may hold values from -6 to 6
Outputs:
- mixed_out: bfloat16 [4096, 2048], P(('groups', 'context'), 'tensor'), parts along dimension 0
The draws below stay inside these ranges and needn't reach their ends.
There are 2 independent parts, one for each index of `groups`. The reference program is written for one: setup_inputs(seed, part) draws one part's arguments, and reference() takes and returns one part's arrays. A program takes and returns all parts, laid end to end along the dimension named above; an argument that names none is the same for every part. Nothing has to cross between parts.
All inputs are finite; a program needn't handle non-finite values.
Results may differ from the reference program's by a relative error of at most 0.0074.
Values may be sent and summed in bfloat16 or wider, within the bound.
No kernel may reach another device: no remote copies, remote signals or barrier semaphores. Data moves between devices by JAX's collectives and lax.ppermute only.
A program may use at most 128 MiB of HBM per device.

```python
import math
import jax
import jax.numpy as jnp
from jax import lax

D = 4096
POLES = 16
CH = 2048
KERNEL = 7
TOKENS = 2048


def shard_levels(own_key, shape, cuts, least, largest):
    loudness = 1.0
    for axis_at, parts in cuts:
        steps = jax.random.uniform(jax.random.fold_in(jax.random.fold_in(own_key, 6), axis_at), (parts,), jnp.float32, least / len(cuts), largest / len(cuts))
        loudness = loudness * jnp.repeat(jnp.exp(steps), shape[axis_at] // parts).reshape((-1,) + (1,) * (len(shape) - 1 - axis_at))
    return loudness


def scatter_about(stream_key, extent, deviation, reach, pieces=(), dtype=jnp.bfloat16):
    values = deviation * jax.random.normal(stream_key, extent, jnp.float32)
    if pieces:
        values = values * shard_levels(stream_key, extent, pieces, -0.22, 0.18)
    return jnp.clip(values, -reach, reach).astype(dtype)


def setup_inputs(seed: int = 0, part: int = 0) -> dict:
    keys = jax.random.split(jax.random.key(seed), 10)
    own_keys = jax.random.split(jax.random.fold_in(keys[9], part), 10)
    hidden = scatter_about(own_keys[0], (TOKENS, D), 1.0, 6.0, ((0, 4), (1, 4)))
    norm_gain = jnp.clip(1.0 + 0.18 * jax.random.normal(keys[1], (D,), jnp.float32), 0.1, 1.9)
    in_proj = scatter_about(keys[2], (D, 3, CH), D ** -0.5, 0.09375, ((2, 4),))
    short_filter = scatter_about(keys[3], (KERNEL, 3, CH), KERNEL ** -0.5, 2.0, ((2, 4),), jnp.float32)
    conv_cache = scatter_about(own_keys[4], (KERNEL - 1, 3, CH), 1.0, 6.0, ((2, 4),))
    decay = jnp.clip(jnp.exp(math.log(0.05) - 8.54091 * jax.random.uniform(keys[5], (CH, POLES), jnp.float32) ** shard_levels(keys[5], (CH, POLES), ((0, 4),), -0.2, 0.2)), 9.765624781721272e-06, 0.05)
    residues = scatter_about(keys[6], (CH, POLES), 0.3, 4.0, ((0, 4),), jnp.float32)
    skip_gain = scatter_about(keys[7], (CH,), 0.5, 6.0, ((0, 4),), jnp.float32)
    cached_state = scatter_about(own_keys[8], (CH, POLES), 1.0, 6.0, ((0, 4),), jnp.float32)
    return dict(hidden=hidden, norm_gain=norm_gain, in_proj=in_proj, short_filter=short_filter, conv_cache=conv_cache, decay=decay, residues=residues, skip_gain=skip_gain, cached_state=cached_state)


EPS = 1e-06

def reference(hidden, norm_gain, in_proj, short_filter, conv_cache, decay, residues, skip_gain, cached_state):
    rows = hidden.astype(jnp.float32)
    scale = lax.rsqrt(lax.optimization_barrier(jnp.mean(rows * rows, axis=1, keepdims=True)) + EPS)
    normed = (rows * scale * norm_gain).astype(jnp.bfloat16)
    width = in_proj.shape[0]
    channels = in_proj.shape[2]
    flat = jnp.dot(normed, in_proj.reshape(width, 3 * channels), preferred_element_type=jnp.float32)
    streams = flat.reshape(-1, 3, channels).astype(jnp.bfloat16)
    extended = jnp.concatenate([conv_cache, streams], axis=0).astype(jnp.float32)
    count = streams.shape[0]
    featured = jnp.zeros((count, 3, channels), jnp.float32)
    for offset in range(short_filter.shape[0]):
        featured = featured + short_filter[offset] * extended[offset:offset + count]
    query = featured[:, 0]
    product = featured[:, 1] * featured[:, 2]
    factor = jnp.exp(-decay)
    inject = jnp.sqrt(-jnp.expm1(-2.0 * decay))

    def advance(state, entry):
        state = factor * state + inject * entry[:, None]
        return (state, lax.optimization_barrier(jnp.sum(residues * state, axis=1)))
    unused, long_out = lax.scan(advance, cached_state, product)
    result = query * (long_out + skip_gain * product)
    return result.astype(jnp.bfloat16)
```

```python
import functools

import jax
import jax.numpy as jnp
from jax import lax
from jax.experimental import pallas as pl
from jax.experimental.pallas import tpu as pltpu
from jax.sharding import PartitionSpec as P

D = 4096
EPS = 1e-06
LANES = 128
SEGS = 8
TAIL = 16
HALO = 8

VM = pl.BlockSpec(memory_space=pltpu.VMEM)
F32 = jnp.float32
BF16 = jnp.bfloat16


def shifted(block, axis, distance):
    size = lax.axis_size(axis)
    return lax.ppermute(block, axis, [(i - distance, i) for i in range(distance, size)])


def flipped(block, bit):
    size = lax.axis_size("tensor")
    return lax.ppermute(block, "tensor", [(i, i ^ bit) for i in range(size)])


def call(kernel, outs, scratch, args, flops=0, limit=12):
    return pl.pallas_call(
        kernel,
        out_shape=outs,
        in_specs=[VM] * len(args),
        out_specs=jax.tree.map(lambda _: VM, outs),
        scratch_shapes=scratch,
        cost_estimate=pl.CostEstimate(flops=flops, bytes_accessed=1 << 20, transcendentals=0),
        compiler_params=pltpu.CompilerParams(vmem_limit_bytes=limit << 20),
    )(*args)


def sds(*shape, dtype=F32):
    return jax.ShapeDtypeStruct(shape, dtype)


def table_kernel(seg, chunks, dec_ref, res_ref, inj_ref, fac_ref, rin_ref, scan_ref, span_ref, end_ref, reach_ref):
    groups, poles = fac_ref.shape[0], fac_ref.shape[1]
    row = lax.broadcasted_iota(jnp.int32, (SEGS, LANES), 0)
    rowf = row.astype(F32)

    def body(g, c):
        lanes = pl.ds(pl.multiple_of(g * LANES, LANES), LANES)
        for n in range(poles):
            dec = jnp.broadcast_to(dec_ref[n : n + 1, lanes], (SEGS, LANES))
            res = jnp.broadcast_to(res_ref[n : n + 1, lanes], (SEGS, LANES))
            inj = jnp.broadcast_to(inj_ref[n : n + 1, lanes], (SEGS, LANES))
            fac_ref[g, n] = jnp.exp(-dec)
            rin_ref[g, n] = res * inj
            for b, step in enumerate((1, 2, 4)):
                scan_ref[b, g, n] = jnp.where(row >= step, jnp.exp(-dec * float(seg * step)), 0.0)
            span_ref[g, n] = jnp.exp(-dec * float(seg * SEGS))
            end_ref[g, n] = jnp.exp(-dec * ((SEGS - 1.0 - rowf) * float(seg)))
            for k in range(chunks):
                reach_ref[k, g, n] = res * jnp.exp(-dec * (1.0 + float(seg) * (float(SEGS * k) + rowf)))
        return c

    lax.fori_loop(0, groups, body, 0)


def project(start, rows, h_ref, sib_ref, far_ref, fwd_ref, gain_ref, w_ref, ext_ref, normed_ref):
    t = lax.axis_index("tensor")
    width = h_ref.shape[1]
    groups = ext_ref.shape[0] // 3
    blocks = (
        (t, lambda: h_ref[start : start + rows, :]),
        (t ^ 1, lambda: sib_ref[start : start + rows, :]),
        (t ^ 2, lambda: far_ref[...]),
        (t ^ 3, lambda: fwd_ref[...]),
    )
    squares = jnp.zeros((rows, LANES), F32)
    for _, load in blocks:
        block = load().astype(F32)
        block = block * block
        for at in range(0, width, LANES):
            squares = squares + block[:, at : at + LANES]
    scale = lax.rsqrt(jnp.sum(squares, axis=1, keepdims=True) / D + EPS)
    for index, load in blocks:
        lanes = pl.ds(pl.multiple_of(index * width, width), width)
        normed_ref[:, lanes] = (load().astype(F32) * scale * gain_ref[:, lanes]).astype(BF16)

    halves = groups // 2

    def body(step, c):
        i, half = step // halves, step % halves
        lanes = pl.ds(pl.multiple_of(half * 2 * LANES, 2 * LANES), 2 * LANES)
        streams = jnp.dot(normed_ref[...], w_ref[i, :, lanes], preferred_element_type=F32)
        streams = streams.astype(BF16).astype(F32)
        ext_ref[step * 2, HALO : HALO + rows, :] = streams[:, :LANES]
        ext_ref[step * 2 + 1, HALO : HALO + rows, :] = streams[:, LANES:]
        return c

    lax.fori_loop(0, 3 * halves, body, 0)


def convolve(ext_ref, filt_ref, g, tokens):
    groups = ext_ref.shape[0] // 3
    lanes = pl.ds(pl.multiple_of(g * LANES, LANES), LANES)
    taps = filt_ref.shape[1]
    found = []
    for i in range(3):
        total = jnp.zeros((tokens, LANES), F32)
        for k in range(taps):
            rows = pl.ds(HALO - taps + 1 + k, tokens)
            total = total + filt_ref[i, k : k + 1, lanes] * ext_ref[i * groups + g, rows, :]
        found.append(total)
    return found


def scan_chunk(prod_ref, fac_ref, rin_ref, g, seg, out_ref):
    poles = fac_ref.shape[1]
    entry = prod_ref[g, pl.ds(0, SEGS, stride=seg), :]
    state = [entry] * poles
    for j in range(seg):
        if j:
            entry = prod_ref[g, pl.ds(j, SEGS, stride=seg), :]
            state = [fac_ref[g, n] * state[n] + entry for n in range(poles)]
        if out_ref is not None:
            terms = [rin_ref[g, n] * state[n] for n in range(poles)]
            while len(terms) > 1:
                terms = [a + b for a, b in zip(terms[::2], terms[1::2])]
            out_ref[g, pl.ds(j, SEGS, stride=seg), :] = terms[0]
    return state


def tail_kernel(start, h_ref, sib_ref, far_ref, fwd_ref, gain_ref, w_ref, tail_ref, send_ref, ext_ref, normed_ref):
    project(start, TAIL, h_ref, sib_ref, far_ref, fwd_ref, gain_ref, w_ref, ext_ref, normed_ref)
    tail_ref[...] = ext_ref[:, HALO:, :]
    send_ref[...] = ext_ref[:, TAIL:, :].astype(BF16)


def chunk_kernel(
    start, rows, seg, first,
    h_ref, sib_ref, far_ref, fwd_ref, gain_ref, w_ref, filt_ref, fac_ref, rin_ref, span_ref, skip_ref,
    prior_ref, other_ref,
    q_ref, z_ref, ends_ref, sum_ref, last_ref,
    ext_ref, normed_ref, prod_ref,
):
    groups, poles = fac_ref.shape[0], fac_ref.shape[1]
    if first:
        got = prior_ref[...].astype(F32)
        ext_ref[:, :HALO, :] = jnp.where(lax.axis_index("context") == 0, other_ref[...], got)
    else:
        ext_ref[:, :HALO, :] = prior_ref[...]
    project(start, rows, h_ref, sib_ref, far_ref, fwd_ref, gain_ref, w_ref, ext_ref, normed_ref)
    last_ref[...] = ext_ref[:, rows:, :]

    def body(g, c):
        query, keyed, value = convolve(ext_ref, filt_ref, g, rows)
        q_ref[g] = query
        prod_ref[g] = keyed * value
        state = scan_chunk(prod_ref, fac_ref, rin_ref, g, seg, z_ref)
        for n in range(poles):
            ends_ref[g, n] = state[n]
            if first:
                sum_ref[g, n] = state[n]
            else:
                sum_ref[g, n] = span_ref[g, n] * other_ref[g, n] + state[n]
        lanes = pl.ds(pl.multiple_of(g * LANES, LANES), LANES)
        z_ref[g] = z_ref[g] + skip_ref[:, lanes] * prod_ref[g]
        return c

    lax.fori_loop(0, groups, body, 0)


def last_kernel(
    start, rows, seg,
    h_ref, sib_ref, far_ref, fwd_ref, gain_ref, w_ref, filt_ref, fac_ref, span_ref, end_ref,
    prior_ref, sums_ref, tail_ref,
    q_ref, p_ref, end_state_ref,
    ext_ref, normed_ref,
):
    groups, poles = fac_ref.shape[0], fac_ref.shape[1]
    ext_ref[:, :HALO, :] = prior_ref[...]
    project(start, rows, h_ref, sib_ref, far_ref, fwd_ref, gain_ref, w_ref, ext_ref, normed_ref)
    ext_ref[:, HALO + rows :, :] = tail_ref[...]

    def body(g, c):
        query, keyed, value = convolve(ext_ref, filt_ref, g, rows + TAIL)
        q_ref[g] = query
        p_ref[g] = keyed * value
        state = scan_chunk(p_ref, fac_ref, None, g, seg, None)
        for n in range(poles):
            whole = end_ref[g, n] * (span_ref[g, n] * sums_ref[g, n] + state[n])
            end_state_ref[pl.ds(g * poles + n, 1), :] = jnp.sum(whole, axis=0, keepdims=True)
        return c

    lax.fori_loop(0, groups, body, 0)


def starts_kernel(chunks, seg, fac_ref, rin_ref, scan_ref, skip_ref, p_ref, *refs):
    ends_refs = refs[: chunks - 1]
    z_ref, begin_ref = refs[chunks - 1 :]
    groups, poles = fac_ref.shape[0], fac_ref.shape[1]
    row = lax.broadcasted_iota(jnp.int32, (SEGS, LANES), 0)

    def body(g, c):
        state = scan_chunk(p_ref, fac_ref, rin_ref, g, seg, z_ref)
        lanes = pl.ds(pl.multiple_of(g * LANES, LANES), LANES)
        z_ref[g] = z_ref[g] + skip_ref[:, lanes] * p_ref[g]
        for n in range(poles):
            lead = rin_ref[g, n] * fac_ref[g, n]
            step = jnp.broadcast_to(scan_ref[0, g, n, 1:2, :], (SEGS, LANES))
            enter = jnp.zeros((SEGS, LANES), F32)
            for k in range(chunks):
                held = ends_refs[k][g, n] if k < chunks - 1 else state[n]
                held = jnp.where(row == 0, held + step * enter, held)
                for b, by in enumerate((1, 2, 4)):
                    held = held + scan_ref[b, g, n] * pltpu.roll(held, by, 0)
                begin_ref[k, g, n] = lead * jnp.where(row == 0, enter, pltpu.roll(held, 1, 0))
                enter = jnp.broadcast_to(held[SEGS - 1 :, :], (SEGS, LANES))
        return c

    lax.fori_loop(0, groups, body, 0)


def final_kernel(chunks, seg, hops, fac_ref, reach_ref, begin_ref, inj_ref, from_cache_ref, jump_ref, *refs):
    e_refs = refs[:hops]
    q_refs = refs[hops : hops + chunks]
    z_refs = refs[hops + chunks : hops + 2 * chunks]
    out_ref, add_ref, enter_ref = refs[hops + 2 * chunks :]
    groups, poles = fac_ref.shape[0], fac_ref.shape[1]
    tokens = seg * SEGS

    for g in range(groups):
        lanes = slice(g * LANES, (g + 1) * LANES)
        total = e_refs[hops - 1][g * poles : (g + 1) * poles, :]
        for e in reversed(range(hops - 1)):
            total = total * jump_ref[:, lanes] + e_refs[e][g * poles : (g + 1) * poles, :]
        enter_ref[g] = inj_ref[:, lanes] * total + from_cache_ref[:, lanes]

    def body(step, c):
        k, g = step // groups, step % groups
        state = []
        for n in range(poles):
            enter = jnp.broadcast_to(enter_ref[g, n : n + 1, :], (SEGS, LANES))
            state.append(begin_ref[k, g, n] + reach_ref[k, g, n] * enter)
        for j in range(seg):
            if j:
                state = [fac_ref[g, n] * state[n] for n in range(poles)]
            terms = state
            while len(terms) > 1:
                terms = [a + b for a, b in zip(terms[::2], terms[1::2])]
            add_ref[step, pl.ds(j, SEGS, stride=seg), :] = terms[0]
        return c

    lax.fori_loop(0, chunks * groups, body, 0)
    for k in range(chunks):
        for g in range(groups):
            out_ref[k * tokens : (k + 1) * tokens, g * LANES : (g + 1) * LANES] = (
                q_refs[k][g] * (z_refs[k][g] + add_ref[k * groups + g])
            ).astype(BF16)


def local(
    hidden, norm_gain, in_proj, short_filter, conv_cache, decay, residues, skip_gain, cached_state
):
    count, width = hidden.shape
    chans = in_proj.shape[2]
    poles = decay.shape[1]
    taps = short_filter.shape[0]
    groups = chans // LANES
    chunks = 4
    tokens = count // chunks
    seg = tokens // SEGS
    position = lax.axis_index("context").astype(F32)
    contexts = lax.axis_size("context")

    bounds = [(count - TAIL, TAIL)]
    for k in range(chunks):
        bounds.append((k * tokens, tokens - (TAIL if k == chunks - 1 else 0)))
    far = [flipped(hidden[a : a + n], 2) for a, n in bounds]
    sib = flipped(hidden, 1)
    fwd = [flipped(block, 1) for block in far]

    w = in_proj.transpose(1, 0, 2)
    filt = short_filter.transpose(1, 0, 2)
    gain = norm_gain[None]
    skip = skip_gain[None]
    dec, res = decay.T, residues.T
    inj = jnp.sqrt(-jnp.expm1(-2.0 * dec))
    jump = jnp.exp(-dec * count)
    from_cache = jnp.exp(-dec * (count * position)) * cached_state.T
    tile = (groups, poles, SEGS, LANES)
    fac, rin, scan, span, end, reach = call(
        functools.partial(table_kernel, seg, chunks),
        [sds(*tile), sds(*tile), sds(3, *tile), sds(*tile), sds(*tile), sds(chunks, *tile)],
        [],
        (dec, res, inj),
    )

    def ext(rows):
        return pltpu.VMEM((3 * groups, HALO + rows, LANES), F32)

    halo = (3 * groups, HALO, LANES)
    tail, send = call(
        functools.partial(tail_kernel, count - TAIL),
        [sds(3 * groups, TAIL, LANES), sds(*halo, dtype=BF16)],
        [ext(TAIL), pltpu.VMEM((TAIL, D), BF16)],
        (hidden, sib, far[0], fwd[0], gain, w),
        flops=2 * TAIL * D * 3 * chans,
    )
    prior = shifted(send, "context", 1)
    cache = jnp.pad(conv_cache.astype(F32), ((HALO - taps + 1, 0), (0, 0), (0, 0)))
    other = cache.reshape(HALO, 3 * groups, LANES).transpose(1, 0, 2)

    plane = (groups, tokens, LANES)
    qs, zs, ends = [], [], []
    for k in range(chunks - 1):
        a, n = bounds[1 + k]
        q, z, e, sums, last = call(
            functools.partial(chunk_kernel, a, n, seg, k == 0),
            [sds(*plane), sds(*plane), sds(*tile), sds(*tile), sds(*halo)],
            [ext(n), pltpu.VMEM((n, D), BF16), pltpu.VMEM(plane, F32)],
            (hidden, sib, far[1 + k], fwd[1 + k], gain, w, filt, fac, rin, span, skip, prior, other),
            flops=2 * n * D * 3 * chans,
        )
        qs.append(q)
        zs.append(z)
        ends.append(e)
        prior, other = last, sums
    a, n = bounds[chunks]
    q, p, end_state = call(
        functools.partial(last_kernel, a, n, seg),
        [sds(*plane), sds(*plane), sds(groups * poles, LANES)],
        [ext(tokens), pltpu.VMEM((n, D), BF16)],
        (hidden, sib, far[chunks], fwd[chunks], gain, w, filt, fac, span, end, prior, other, tail),
        flops=2 * n * D * 3 * chans,
    )
    qs.append(q)
    if contexts <= 4:
        before = [shifted(end_state, "context", d) for d in range(1, contexts)]
    else:
        every = lax.all_gather(end_state.reshape(groups, poles, LANES), "context")
        gaps = position - 1.0 - jnp.arange(contexts, dtype=F32)
        rates = dec.reshape(poles, groups, LANES).transpose(1, 0, 2)
        weights = jnp.where(
            (gaps >= 0.0)[:, None, None, None],
            jnp.exp(-rates[None] * count * jnp.maximum(gaps, 0.0)[:, None, None, None]),
            0.0,
        )
        before = [jnp.sum(weights * every, axis=0).reshape(groups * poles, LANES)]
    z, begin = call(
        functools.partial(starts_kernel, chunks, seg),
        [sds(*plane), sds(chunks, *tile)],
        [],
        (fac, rin, scan, skip, p, *ends),
        flops=1 << 30,
    )
    zs.append(z)
    return call(
        functools.partial(final_kernel, chunks, seg, len(before)),
        sds(count, chans, dtype=BF16),
        [pltpu.VMEM((chunks * groups, tokens, LANES), F32), pltpu.VMEM((groups, poles, LANES), F32)],
        (fac, reach, begin, inj, from_cache, jump, *before, *qs, *zs),
    )


def solution(mesh):
    placed = (
        P(("groups", "context"), "tensor"),
        P(),
        P(None, None, "tensor"),
        P(None, None, "tensor"),
        P("groups", None, "tensor"),
        P("tensor", None),
        P("tensor", None),
        P("tensor"),
        P(("groups", "tensor"), None),
    )
    return jax.shard_map(
        local,
        mesh=mesh,
        in_specs=placed,
        out_specs=P(("groups", "context"), "tensor"),
        check_vma=False,
    )
```

```python
import functools

import jax
import jax.numpy as jnp
from jax import lax
from jax.experimental import pallas as pl
from jax.experimental.pallas import tpu as pltpu
from jax.sharding import PartitionSpec as P

D = 4096
EPS = 1e-06
LANES = 128
SEGS = 8
TAIL = 16
HALO = 8

VM = pl.BlockSpec(memory_space=pltpu.VMEM)
F32 = jnp.float32
BF16 = jnp.bfloat16


def shifted(block, axis, distance):
    size = lax.axis_size(axis)
    return lax.ppermute(block, axis, [(i - distance, i) for i in range(distance, size)])


def flipped(block, bit):
    size = lax.axis_size("tensor")
    return lax.ppermute(block, "tensor", [(i, i ^ bit) for i in range(size)])


def call(kernel, outs, scratch, args, flops=0, limit=12, anywhere=()):
    specs = [pl.BlockSpec(memory_space=pltpu.HBM) if i in anywhere else VM for i in range(len(args))]
    args = [pltpu.with_memory_space_constraint(x, pltpu.HBM) if i in anywhere else x for i, x in enumerate(args)]
    return pl.pallas_call(
        kernel,
        out_shape=outs,
        in_specs=specs,
        out_specs=jax.tree.map(lambda _: VM, outs, is_leaf=lambda o: hasattr(o, "dtype")),
        scratch_shapes=scratch,
        cost_estimate=pl.CostEstimate(flops=flops, bytes_accessed=1024, transcendentals=0),
        compiler_params=pltpu.CompilerParams(vmem_limit_bytes=limit << 20),
    )(*args)


def kept(*shape, dtype=F32):
    return pltpu.VMEM(shape, dtype)


def sds(*shape, dtype=F32):
    return jax.ShapeDtypeStruct(shape, dtype)


def open_kernel(pieces, h_any, *refs):
    *out_refs, sem = refs
    copies, which = [], 0
    for parts, out_ref in zip(pieces, out_refs):
        at = 0
        for start, rows in parts:
            copies.append(
                pltpu.make_async_copy(
                    h_any.at[start : start + rows, :], out_ref.at[at : at + rows, :], sem.at[which]
                )
            )
            at += rows
            which += 1
    for copy in copies:
        copy.start()
    for copy in copies:
        copy.wait()


def stage_kernel(
    seg, chunks, w_any, dec_ref, res_ref, inj_ref,
    w_ref, fac_ref, rin_ref, scan_ref, span_ref, end_ref, reach_ref, sem,
):
    copies = [pltpu.make_async_copy(w_any, w_ref, sem.at[0])]
    for copy in copies:
        copy.start()
    groups, poles = fac_ref.shape[0], fac_ref.shape[1]
    row = lax.broadcasted_iota(jnp.int32, (SEGS, LANES), 0)
    rowf = row.astype(F32)

    def body(g, c):
        lanes = pl.ds(pl.multiple_of(g * LANES, LANES), LANES)
        for n in range(poles):
            dec = jnp.broadcast_to(dec_ref[n : n + 1, lanes], (SEGS, LANES))
            res = jnp.broadcast_to(res_ref[n : n + 1, lanes], (SEGS, LANES))
            inj = jnp.broadcast_to(inj_ref[n : n + 1, lanes], (SEGS, LANES))
            fac_ref[g, n] = jnp.exp(-dec)
            rin_ref[g, n] = res * inj
            for b, step in enumerate((1, 2, 4)):
                scan_ref[b, g, n] = jnp.where(row >= step, jnp.exp(-dec * float(seg * step)), 0.0)
            span_ref[g, n] = jnp.exp(-dec * float(seg * SEGS))
            end_ref[g, n] = jnp.exp(-dec * ((SEGS - 1.0 - rowf) * float(seg)))
            for k in range(chunks):
                reach_ref[k, g, n] = res * jnp.exp(-dec * (1.0 + float(seg) * (float(SEGS * k) + rowf)))
        return c

    lax.fori_loop(0, groups, body, 0)
    for copy in copies:
        copy.wait()


def project(parts, h_ref, sib_ref, far_ref, fwd_ref, gain_ref, w_ref, normed_ref, put):
    t = lax.axis_index("tensor")
    width = h_ref.shape[1]
    groups = w_ref.shape[2] // LANES
    at = 0
    for start, rows in parts:
        here = slice(at, at + rows)
        at += rows
        blocks = (
            (t, h_ref, here),
            (t ^ 1, sib_ref, slice(start, start + rows)),
            (t ^ 2, far_ref, here),
            (t ^ 3, fwd_ref, here),
        )
        squares = jnp.zeros((rows, LANES), F32)
        for _, ref, where in blocks:
            block = ref[where, :].astype(F32)
            block = block * block
            for lane in range(0, width, LANES):
                squares = squares + block[:, lane : lane + LANES]
        scale = lax.rsqrt(jnp.sum(squares, axis=1, keepdims=True) / D + EPS)
        for index, ref, where in blocks:
            lanes = pl.ds(pl.multiple_of(index * width, width), width)
            normed_ref[here, lanes] = (ref[where, :].astype(F32) * scale * gain_ref[:, lanes]).astype(BF16)

    halves = groups // 2

    def body(step, c):
        i, half = step // halves, step % halves
        lanes = pl.ds(pl.multiple_of(half * 2 * LANES, 2 * LANES), 2 * LANES)
        streams = jnp.dot(normed_ref[...], w_ref[i, :, lanes], preferred_element_type=F32)
        streams = streams.astype(BF16).astype(F32)
        put(step * 2, streams[:, :LANES])
        put(step * 2 + 1, streams[:, LANES:])
        return c

    lax.fori_loop(0, 3 * halves, body, 0)


def convolve(ext_ref, filt_ref, g, first, tokens, streams=(0, 1, 2)):
    groups = ext_ref.shape[0] // 3
    lanes = pl.ds(pl.multiple_of(g * LANES, LANES), LANES)
    taps = filt_ref.shape[1]
    found = []
    for i in streams:
        total = jnp.zeros((tokens, LANES), F32)
        for k in range(taps):
            rows = pl.ds(first + HALO - taps + 1 + k, tokens)
            total = total + filt_ref[i, k : k + 1, lanes] * ext_ref[i * groups + g, rows, :]
        found.append(total)
    return found


def scan_unit(prod_ref, fac_ref, rin_ref, g, first, seg, out_ref):
    poles = fac_ref.shape[1]
    entry = prod_ref[g, pl.ds(first, SEGS, stride=seg), :]
    state = [entry] * poles
    for j in range(seg):
        rows = pl.ds(first + j, SEGS, stride=seg)
        if j:
            entry = prod_ref[g, rows, :]
            state = [fac_ref[g, n] * state[n] + entry for n in range(poles)]
        if out_ref is not None:
            terms = [rin_ref[g, n] * state[n] for n in range(poles)]
            while len(terms) > 1:
                terms = [a + b for a, b in zip(terms[::2], terms[1::2])]
            out_ref[g, rows, :] = terms[0]
    return state


def head_kernel(
    parts, h_ref, sib_ref, far_ref, fwd_ref, gain_ref, w_ref, tail_ref, send_ref, body_ref, normed_ref
):
    def put(at, streams):
        tail_ref[at] = streams[:TAIL]
        send_ref[at] = streams[TAIL - HALO : TAIL].astype(BF16)
        body_ref[at] = streams[TAIL:]

    project(parts, h_ref, sib_ref, far_ref, fwd_ref, gain_ref, w_ref, normed_ref, put)


def chunk_kernel(
    parts, units, seg, first,
    h_ref, sib_ref, far_ref, fwd_ref, gain_ref, w_ref, filt_ref, fac_ref, rin_ref, span_ref, skip_ref,
    prior_ref, other_ref, body_ref,
    q_ref, z_ref, ends_ref, sum_ref, last_ref,
    ext_ref, normed_ref, prod_ref,
):
    groups, poles = fac_ref.shape[0], fac_ref.shape[1]
    tokens = seg * SEGS
    base = HALO
    if first:
        got = prior_ref[...].astype(F32)
        ext_ref[:, :HALO, :] = jnp.where(lax.axis_index("context") == 0, other_ref[...], got)
        base += body_ref.shape[1]
        ext_ref[:, HALO:base, :] = body_ref[...]
    else:
        ext_ref[:, :HALO, :] = prior_ref[...]
    rows = sum(n for _, n in parts)

    def put(at, streams):
        ext_ref[at, base : base + rows, :] = streams

    project(parts, h_ref, sib_ref, far_ref, fwd_ref, gain_ref, w_ref, normed_ref, put)
    last_ref[...] = ext_ref[:, base + rows - HALO :, :]

    def body(g, c):
        lanes = pl.ds(pl.multiple_of(g * LANES, LANES), LANES)
        for u in range(units):
            here = slice(u * tokens, (u + 1) * tokens)
            query, keyed, value = convolve(ext_ref, filt_ref, g, u * tokens, tokens)
            q_ref[g, here, :] = query
            prod_ref[g, here, :] = keyed * value
            state = scan_unit(prod_ref, fac_ref, rin_ref, g, u * tokens, seg, z_ref)
            for n in range(poles):
                ends_ref[u, g, n] = state[n]
                if u:
                    sum_ref[g, n] = span_ref[g, n] * sum_ref[g, n] + state[n]
                elif first:
                    sum_ref[g, n] = state[n]
                else:
                    sum_ref[g, n] = span_ref[g, n] * other_ref[g, n] + state[n]
        z_ref[g] = z_ref[g] + skip_ref[:, lanes] * prod_ref[g]
        return c

    lax.fori_loop(0, groups, body, 0)


def last_kernel(
    parts, seg,
    h_ref, sib_ref, far_ref, fwd_ref, gain_ref, w_ref, filt_ref, fac_ref, span_ref, end_ref,
    prior_ref, sums_ref, tail_ref,
    q_ref, p_ref, end_state_ref,
    ext_ref, normed_ref,
):
    groups, poles = fac_ref.shape[0], fac_ref.shape[1]
    rows = sum(n for _, n in parts)
    ext_ref[:, :HALO, :] = prior_ref[...]

    def put(at, streams):
        ext_ref[at, HALO : HALO + rows, :] = streams

    project(parts, h_ref, sib_ref, far_ref, fwd_ref, gain_ref, w_ref, normed_ref, put)
    ext_ref[:, HALO + rows :, :] = tail_ref[...]

    def body(g, c):
        query, keyed, value = convolve(ext_ref, filt_ref, g, 0, rows + TAIL)
        q_ref[g] = query
        p_ref[g] = keyed * value
        state = scan_unit(p_ref, fac_ref, None, g, 0, seg, None)
        for n in range(poles):
            whole = end_ref[g, n] * (span_ref[g, n] * sums_ref[g, n] + state[n])
            end_state_ref[pl.ds(g * poles + n, 1), :] = jnp.sum(whole, axis=0, keepdims=True)
        return c

    lax.fori_loop(0, groups, body, 0)


def starts_kernel(chunks, seg, fac_ref, rin_ref, scan_ref, skip_ref, p_ref, *refs):
    *ends_refs, z_ref, begin_ref = refs
    ends_refs = [ref.at[u] for ref in ends_refs for u in range(ref.shape[0])]
    groups, poles = fac_ref.shape[0], fac_ref.shape[1]
    row = lax.broadcasted_iota(jnp.int32, (SEGS, LANES), 0)

    def body(g, c):
        state = scan_unit(p_ref, fac_ref, rin_ref, g, 0, seg, z_ref)
        lanes = pl.ds(pl.multiple_of(g * LANES, LANES), LANES)
        z_ref[g] = z_ref[g] + skip_ref[:, lanes] * p_ref[g]
        for n in range(poles):
            lead = rin_ref[g, n] * fac_ref[g, n]
            step = jnp.broadcast_to(scan_ref[0, g, n, 1:2, :], (SEGS, LANES))
            enter = jnp.zeros((SEGS, LANES), F32)
            for k in range(chunks):
                held = ends_refs[k][g, n] if k < chunks - 1 else state[n]
                held = jnp.where(row == 0, held + step * enter, held)
                for b, by in enumerate((1, 2, 4)):
                    held = held + scan_ref[b, g, n] * pltpu.roll(held, by, 0)
                begin_ref[k, g, n] = lead * jnp.where(row == 0, enter, pltpu.roll(held, 1, 0))
                enter = jnp.broadcast_to(held[SEGS - 1 :, :], (SEGS, LANES))
        return c

    lax.fori_loop(0, groups, body, 0)


def final_kernel(
    chunks, seg, hops, pieces, wrapped, fac_ref, reach_ref, begin_ref, inj_ref, from_cache_ref, jump_ref, *refs
):
    e_refs = refs[:hops]
    q_refs = refs[hops : hops + pieces]
    z_refs = refs[hops + pieces : hops + 2 * pieces]
    out_ref, add_ref, enter_ref = refs[hops + 2 * pieces :]
    groups, poles = fac_ref.shape[0], fac_ref.shape[1]
    tokens = seg * SEGS
    position = lax.axis_index("context")

    def before(e, rows):
        found = e_refs[e][rows, :]
        return jnp.where(position > e, found, 0.0) if wrapped else found

    for g in range(groups):
        lanes = slice(g * LANES, (g + 1) * LANES)
        rows = slice(g * poles, (g + 1) * poles)
        total = before(hops - 1, rows)
        for e in reversed(range(hops - 1)):
            total = total * jump_ref[:, lanes] + before(e, rows)
        enter_ref[g] = inj_ref[:, lanes] * total + from_cache_ref[:, lanes]

    def body(step, c):
        k, g = step // groups, step % groups
        state = []
        for n in range(poles):
            enter = jnp.broadcast_to(enter_ref[g, n : n + 1, :], (SEGS, LANES))
            state.append(begin_ref[k, g, n] + reach_ref[k, g, n] * enter)
        for j in range(seg):
            if j:
                state = [fac_ref[g, n] * state[n] for n in range(poles)]
            terms = state
            while len(terms) > 1:
                terms = [a + b for a, b in zip(terms[::2], terms[1::2])]
            add_ref[step, pl.ds(j, SEGS, stride=seg), :] = terms[0]
        return c

    lax.fori_loop(0, chunks * groups, body, 0)
    k = 0
    for q_ref, z_ref in zip(q_refs, z_refs):
        for u in range(q_ref.shape[1] // tokens):
            here = slice(u * tokens, (u + 1) * tokens)
            for g in range(groups):
                out_ref[k * tokens : (k + 1) * tokens, g * LANES : (g + 1) * LANES] = (
                    q_ref[g, here, :] * (z_ref[g, here, :] + add_ref[k * groups + g])
                ).astype(BF16)
            k += 1


def local(
    hidden, norm_gain, in_proj, short_filter, conv_cache, decay, residues, skip_gain, cached_state
):
    count, width = hidden.shape
    chans = in_proj.shape[2]
    poles = decay.shape[1]
    taps = short_filter.shape[0]
    groups = chans // LANES
    chunks = 4
    tokens = count // chunks
    seg = tokens // SEGS
    position = lax.axis_index("context").astype(F32)
    contexts = lax.axis_size("context")

    head = [(count - TAIL, TAIL), (0, tokens)]
    rest = [[(k * tokens, tokens - (TAIL if k == chunks - 1 else 0))] for k in range(1, chunks)]
    own = call(
        functools.partial(open_kernel, [head] + rest),
        [kept(sum(n for _, n in parts), width, dtype=BF16) for parts in [head] + rest],
        [pltpu.SemaphoreType.DMA((chunks + 1,))],
        (hidden,),
        anywhere=(0,),
    )
    hidden, own = lax.optimization_barrier((hidden, own))
    far = [flipped(block, 2) for block in own]
    sib = flipped(hidden, 1)

    filt = short_filter.transpose(1, 0, 2)
    gain = norm_gain[None]
    skip = skip_gain[None]
    dec, res = decay.T, residues.T
    inj = jnp.sqrt(-jnp.expm1(-2.0 * dec))
    jump = jnp.exp(-dec * count)
    from_cache = jnp.exp(-dec * (count * position)) * cached_state.T
    cache = jnp.pad(conv_cache.astype(F32), ((HALO - taps + 1, 0), (0, 0), (0, 0)))
    cache = cache.reshape(HALO, 3 * groups, LANES).transpose(1, 0, 2)
    tile = (groups, poles, SEGS, LANES)
    w = in_proj.transpose(1, 0, 2)
    w, inj, jump, from_cache, cache = lax.optimization_barrier((w, inj, jump, from_cache, cache))
    w, fac, rin, scan, span, end, reach = call(
        functools.partial(stage_kernel, seg, chunks),
        [
            kept(*w.shape, dtype=BF16), kept(*tile), kept(*tile),
            kept(3, *tile), kept(*tile), kept(*tile), kept(chunks, *tile),
        ],
        [pltpu.SemaphoreType.DMA((1,))],
        (w, dec, res, inj),
        anywhere=(0,),
    )

    def ext(rows):
        return pltpu.VMEM((3 * groups, HALO + rows, LANES), F32)

    halo = (3 * groups, HALO, LANES)
    work = 2 * D * 3 * chans
    fwd = flipped(far[0], 1)
    tail, send, body = call(
        functools.partial(head_kernel, head),
        [sds(3 * groups, TAIL, LANES), sds(*halo, dtype=BF16), sds(3 * groups, tokens, LANES)],
        [pltpu.VMEM((TAIL + tokens, D), BF16)],
        (own[0], sib, far[0], fwd, gain, w),
    )
    prior, other, after = shifted(send, "context", 1), cache, body
    qs, zs, ends = [], [], []
    for k in range(1, chunks - 1):
        (n,) = [n for _, n in rest[k - 1]]
        units = 2 if k == 1 else 1
        plane = (groups, units * tokens, LANES)
        arrived, after = lax.optimization_barrier((far[k], after))
        fwd = flipped(arrived, 1)
        q, z, e, sums, last = call(
            functools.partial(chunk_kernel, rest[k - 1], units, seg, k == 1),
            [sds(*plane), sds(*plane), sds(units, *tile), sds(*tile), sds(*halo)],
            [ext(units * tokens), pltpu.VMEM((n, D), BF16), pltpu.VMEM(plane, F32)],
            (own[k], sib, arrived, fwd, gain, w, filt, fac, rin, span, skip, prior, other, body),
            )
        qs.append(q)
        zs.append(z)
        ends.append(e)
        prior, other, after = last, sums, last
    ((a, n),) = rest[-1]
    plane = (groups, tokens, LANES)
    arrived, after = lax.optimization_barrier((far[-1], after))
    fwd = flipped(arrived, 1)
    q, p, end_state = call(
        functools.partial(last_kernel, rest[-1], seg),
        [sds(*plane), sds(*plane), sds(groups * poles, LANES)],
        [ext(tokens), pltpu.VMEM((n, D), BF16)],
        (own[-1], sib, arrived, fwd, gain, w, filt, fac, span, end, prior, other, tail),
    )
    qs.append(q)
    wrapped = contexts <= 4
    if wrapped:
        before = [
            lax.ppermute(end_state, "context", [(i, (i + d) % contexts) for i in range(contexts)])
            for d in range(1, contexts)
        ]
    else:
        every = lax.all_gather(end_state.reshape(groups, poles, LANES), "context")
        gaps = position - 1.0 - jnp.arange(contexts, dtype=F32)
        rates = dec.reshape(poles, groups, LANES).transpose(1, 0, 2)
        weights = jnp.where(
            (gaps >= 0.0)[:, None, None, None],
            jnp.exp(-rates[None] * count * jnp.maximum(gaps, 0.0)[:, None, None, None]),
            0.0,
        )
        before = [jnp.sum(weights * every, axis=0).reshape(groups * poles, LANES)]
    z, begin = call(
        functools.partial(starts_kernel, chunks, seg),
        [sds(*plane), sds(chunks, *tile)],
        [],
        (fac, rin, scan, skip, p, *ends),
    )
    zs.append(z)
    return call(
        functools.partial(final_kernel, chunks, seg, len(before), len(qs), wrapped),
        sds(count, chans, dtype=BF16),
        [pltpu.VMEM((chunks * groups, tokens, LANES), F32), pltpu.VMEM((groups, poles, LANES), F32)],
        (fac, reach, begin, inj, from_cache, jump, *before, *qs, *zs),
    )


def solution(mesh):
    placed = (
        P(("groups", "context"), "tensor"),
        P(),
        P(None, None, "tensor"),
        P(None, None, "tensor"),
        P("groups", None, "tensor"),
        P("tensor", None),
        P("tensor", None),
        P("tensor"),
        P(("groups", "tensor"), None),
    )
    return jax.shard_map(
        local,
        mesh=mesh,
        in_specs=placed,
        out_specs=P(("groups", "context"), "tensor"),
        check_vma=False,
    )
```

```python
import functools

import jax
import jax.numpy as jnp
from jax import lax
from jax.experimental import pallas as pl
from jax.experimental.pallas import tpu as pltpu
from jax.sharding import PartitionSpec as P

D = 4096
EPS = 1e-06
LANES = 128
SEGS = 8
TAIL = 16
HALO = 8
NOTES = 16

VM = pl.BlockSpec(memory_space=pltpu.VMEM)
F32 = jnp.float32
BF16 = jnp.bfloat16


def shifted(block, axis, distance):
    size = lax.axis_size(axis)
    return lax.ppermute(block, axis, [(i - distance, i) for i in range(distance, size)])


def flipped(block, bit):
    size = lax.axis_size("tensor")
    return lax.ppermute(block, "tensor", [(i, i ^ bit) for i in range(size)])


def call(kernel, outs, scratch, args, flops=0, limit=12, anywhere=()):
    specs = [pl.BlockSpec(memory_space=pltpu.HBM) if i in anywhere else VM for i in range(len(args))]
    args = [pltpu.with_memory_space_constraint(x, pltpu.HBM) if i in anywhere else x for i, x in enumerate(args)]
    return pl.pallas_call(
        kernel,
        out_shape=outs,
        in_specs=specs,
        out_specs=jax.tree.map(lambda _: VM, outs, is_leaf=lambda o: hasattr(o, "dtype")),
        scratch_shapes=scratch,
        cost_estimate=pl.CostEstimate(flops=flops, bytes_accessed=1024, transcendentals=0),
        compiler_params=pltpu.CompilerParams(vmem_limit_bytes=limit << 20),
    )(*args)


def kept(*shape, dtype=F32):
    return pltpu.VMEM(shape, dtype)


def sds(*shape, dtype=F32):
    return jax.ShapeDtypeStruct(shape, dtype)


def open_kernel(pieces, h_any, *refs):
    *out_refs, squares_ref, h_ref, sem = refs
    count, width = h_ref.shape
    whole = pltpu.make_async_copy(h_any, h_ref, sem.at[0])
    whole.start()
    copies = []
    for parts, out_ref in zip(pieces, out_refs):
        at = 0
        for start, rows in parts:
            copies.append(
                pltpu.make_async_copy(
                    h_any.at[start : start + rows, :], out_ref.at[at : at + rows, :], sem.at[1 + len(copies)]
                )
            )
            at += rows
    for copy in copies:
        copy.start()
    whole.wait()
    sums = []
    for at in range(0, count, LANES):
        squares = row_squares(h_ref, slice(at, at + LANES))
        squares_ref[at : at + LANES, :] = squares
        sums.append(jnp.sum(jnp.transpose(squares), axis=0, keepdims=True))
    rest = jnp.concatenate(sums, axis=1)
    terms = []
    for _ in range(3):
        term = rest.astype(BF16).astype(F32)
        rest = rest - term
        terms.append(term)
    coded = jnp.concatenate(terms + [jnp.zeros((NOTES - 3, count), F32)], axis=0).astype(BF16)
    for copy in copies:
        copy.wait()
    first = out_refs[0]
    at = first.shape[0] - NOTES
    first[at:, :count] = coded
    first[at:, count:] = jnp.zeros((NOTES, width - count), BF16)


def row_squares(ref, rows):
    block = ref[rows, :].astype(F32)
    block = block * block
    total = block[:, :LANES]
    for lane in range(LANES, block.shape[1], LANES):
        total = total + block[:, lane : lane + LANES]
    return total


def stage_kernel(
    seg, chunks, w_any, dec_ref, res_ref, inj_ref,
    w_ref, fac_ref, rin_ref, scan_ref, span_ref, end_ref, reach_ref, sem,
):
    copies = [pltpu.make_async_copy(w_any, w_ref, sem.at[0])]
    for copy in copies:
        copy.start()
    groups, poles = fac_ref.shape[0], fac_ref.shape[1]
    row = lax.broadcasted_iota(jnp.int32, (SEGS, LANES), 0)
    rowf = row.astype(F32)

    def body(g, c):
        lanes = pl.ds(pl.multiple_of(g * LANES, LANES), LANES)
        for n in range(poles):
            dec = jnp.broadcast_to(dec_ref[n : n + 1, lanes], (SEGS, LANES))
            res = jnp.broadcast_to(res_ref[n : n + 1, lanes], (SEGS, LANES))
            inj = jnp.broadcast_to(inj_ref[n : n + 1, lanes], (SEGS, LANES))
            fac_ref[g, n] = jnp.exp(-dec)
            rin_ref[g, n] = res * inj
            for b, step in enumerate((1, 2, 4)):
                scan_ref[b, g, n] = jnp.where(row >= step, jnp.exp(-dec * float(seg * step)), 0.0)
            span_ref[g, n] = jnp.exp(-dec * float(seg * SEGS))
            end_ref[g, n] = jnp.exp(-dec * ((SEGS - 1.0 - rowf) * float(seg)))
            for k in range(chunks):
                reach_ref[k, g, n] = res * jnp.exp(-dec * (1.0 + float(seg) * (float(SEGS * k) + rowf)))
        return c

    lax.fori_loop(0, groups, body, 0)
    for copy in copies:
        copy.wait()


def normed_block(ref, rows, scale_ref, start, gain_ref, index):
    width = ref.shape[1]
    lanes = pl.ds(pl.multiple_of(index * width, width), width)
    count = rows.stop - rows.start
    scale = scale_ref[start : start + count, :]
    scale = jnp.concatenate([scale] * (width // LANES), axis=1)
    return (ref[rows, :].astype(F32) * scale * gain_ref[:, lanes]).astype(BF16)


def put_block(normed_ref, rows, index, block):
    width = block.shape[1]
    normed_ref[rows, pl.ds(pl.multiple_of(index * width, width), width)] = block


def multiply(normed_ref, w_ref, start, put):
    groups = w_ref.shape[2] // LANES
    halves = groups // 2
    depth = normed_ref.shape[1]

    def body(step, c):
        i, half = step // halves, step % halves
        lanes = pl.ds(pl.multiple_of(half * 2 * LANES, 2 * LANES), 2 * LANES)
        rows = pl.ds(start, depth)
        products = jnp.dot(normed_ref[...], w_ref[i, rows, lanes], preferred_element_type=F32)
        put(step * 2, products[:, :LANES])
        put(step * 2 + 1, products[:, LANES:])
        return c

    lax.fori_loop(0, 3 * halves, body, 0)


def rounded(streams):
    return streams.astype(BF16).astype(F32)


def convolve(ext_ref, filt_ref, g, first, tokens, streams=(0, 1, 2)):
    groups = ext_ref.shape[0] // 3
    lanes = pl.ds(pl.multiple_of(g * LANES, LANES), LANES)
    taps = filt_ref.shape[1]
    found = []
    for i in streams:
        total = jnp.zeros((tokens, LANES), F32)
        for k in range(taps):
            rows = pl.ds(first + HALO - taps + 1 + k, tokens)
            total = total + filt_ref[i, k : k + 1, lanes] * ext_ref[i * groups + g, rows, :]
        found.append(total)
    return found


def scan_unit(prod_ref, fac_ref, rin_ref, g, first, seg, out_ref):
    poles = fac_ref.shape[1]
    entry = prod_ref[g, pl.ds(first, SEGS, stride=seg), :]
    state = [entry] * poles
    for j in range(seg):
        rows = pl.ds(first + j, SEGS, stride=seg)
        if j:
            entry = prod_ref[g, rows, :]
            state = [fac_ref[g, n] * state[n] + entry for n in range(poles)]
        if out_ref is not None:
            terms = [rin_ref[g, n] * state[n] for n in range(poles)]
            while len(terms) > 1:
                terms = [a + b for a, b in zip(terms[::2], terms[1::2])]
            out_ref[g, rows, :] = terms[0]
    return state


def head_kernel(
    parts, a_ref, sib_ref, far_ref, fwd_ref, squares_ref, gain_ref, w_ref,
    scale_ref, tail_ref, send_ref, body_ref, normed_ref,
):
    t = lax.axis_index("tensor")
    count = squares_ref.shape[0]
    at = far_ref.shape[0] - NOTES
    notes = jnp.zeros((1, count), F32)
    for ref in (far_ref, fwd_ref):
        coded = ref[at:, :count].astype(F32)
        notes = notes + ((coded[0:1] + coded[1:2]) + coded[2:3])
    for row in range(0, count, LANES):
        rows = slice(row, row + LANES)
        others = jnp.transpose(jnp.broadcast_to(notes[:, rows], (LANES, LANES)))
        near = jnp.sum(squares_ref[rows, :] + row_squares(sib_ref, rows), axis=1, keepdims=True)
        scale_ref[rows, :] = lax.rsqrt((near + others) / D + EPS)
    at = 0
    for start, rows in parts:
        here = slice(at, at + rows)
        there = slice(start, start + rows)
        at += rows
        for index, ref, where in ((t, a_ref, here), (t ^ 1, sib_ref, there), (t ^ 2, far_ref, here), (t ^ 3, fwd_ref, here)):
            put_block(normed_ref, here, index, normed_block(ref, where, scale_ref, start, gain_ref, index))

    def put(at, products):
        streams = rounded(products)
        tail_ref[at] = streams[:TAIL]
        send_ref[at] = streams[TAIL - HALO : TAIL].astype(BF16)
        body_ref[at] = streams[TAIL:]

    multiply(normed_ref, w_ref, 0, put)


def near_kernel(parts, *refs):
    own_refs = refs[: len(parts)]
    sib_ref, scale_ref, gain_ref, w_ref, part_ref, normed_ref = refs[len(parts) :]
    t = lax.axis_index("tensor")
    depth = normed_ref.shape[1]
    at = 0
    for own_ref, (start, rows) in zip(own_refs, parts):
        here = slice(at, at + rows)
        at += rows
        own = normed_block(own_ref, slice(0, rows), scale_ref, start, gain_ref, t)
        put_block(normed_ref, here, t & 1, own)
        sib = normed_block(sib_ref, slice(start, start + rows), scale_ref, start, gain_ref, t ^ 1)
        put_block(normed_ref, here, (t & 1) ^ 1, sib)

    def put(at, products):
        part_ref[at] = products

    multiply(normed_ref, w_ref, pl.multiple_of((t >> 1) * depth, depth), put)


def far_part(start, rows, offset, far_ref, fwd_ref, scale_ref, gain_ref, w_ref, part_ref, ext_ref, base, normed_ref):
    t = lax.axis_index("tensor")
    depth = normed_ref.shape[1]
    here = slice(0, rows)
    put_block(normed_ref, here, t & 1, normed_block(far_ref, here, scale_ref, start, gain_ref, t ^ 2))
    put_block(normed_ref, here, (t & 1) ^ 1, normed_block(fwd_ref, here, scale_ref, start, gain_ref, t ^ 3))

    def put(at, products):
        ext_ref[at, base : base + rows, :] = rounded(part_ref[at, offset : offset + rows, :] + products)

    multiply(normed_ref, w_ref, pl.multiple_of(((t >> 1) ^ 1) * depth, depth), put)


def chunk_kernel(
    start, rows, offset, units, seg, first,
    far_ref, fwd_ref, scale_ref, gain_ref, w_ref, part_ref, filt_ref, fac_ref, rin_ref, span_ref, skip_ref,
    prior_ref, other_ref, body_ref,
    q_ref, z_ref, ends_ref, sum_ref, last_ref,
    ext_ref, normed_ref, prod_ref,
):
    groups, poles = fac_ref.shape[0], fac_ref.shape[1]
    tokens = seg * SEGS
    if first:
        got = prior_ref[...].astype(F32)
        ext_ref[:, :HALO, :] = jnp.where(lax.axis_index("context") == 0, other_ref[...], got)
        base = HALO + body_ref.shape[1]
        ext_ref[:, HALO:base, :] = body_ref[...]
    else:
        base = prior_ref.shape[1]
        ext_ref[:, :base, :] = prior_ref[...]
    far_part(start, rows, offset, far_ref, fwd_ref, scale_ref, gain_ref, w_ref, part_ref, ext_ref, base, normed_ref)
    last_ref[...] = ext_ref[:, units * tokens :, :]

    def body(g, c):
        lanes = pl.ds(pl.multiple_of(g * LANES, LANES), LANES)
        query, keyed, value = convolve(ext_ref, filt_ref, g, 0, units * tokens)
        q_ref[g] = query
        prod_ref[g] = keyed * value
        for u in range(units):
            state = scan_unit(prod_ref, fac_ref, rin_ref, g, u * tokens, seg, z_ref)
            for n in range(poles):
                ends_ref[u, g, n] = state[n]
                if u:
                    sum_ref[g, n] = span_ref[g, n] * sum_ref[g, n] + state[n]
                elif first:
                    sum_ref[g, n] = state[n]
                else:
                    sum_ref[g, n] = span_ref[g, n] * other_ref[g, n] + state[n]
        z_ref[g] = z_ref[g] + skip_ref[:, lanes] * prod_ref[g]
        return c

    lax.fori_loop(0, groups, body, 0)


def last_kernel(
    start, rows, offset, units, seg,
    far_ref, fwd_ref, scale_ref, gain_ref, w_ref, part_ref, filt_ref, fac_ref, span_ref, end_ref,
    prior_ref, sums_ref, tail_ref,
    q_ref, p_ref, end_state_ref,
    ext_ref, normed_ref,
):
    groups, poles = fac_ref.shape[0], fac_ref.shape[1]
    tokens = seg * SEGS
    base = prior_ref.shape[1]
    ext_ref[:, :base, :] = prior_ref[...]
    ext_ref[:, base + rows :, :] = tail_ref[...]
    far_part(start, rows, offset, far_ref, fwd_ref, scale_ref, gain_ref, w_ref, part_ref, ext_ref, base, normed_ref)

    def body(g, c):
        query, keyed, value = convolve(ext_ref, filt_ref, g, 0, units * tokens)
        q_ref[g] = query
        p_ref[g] = keyed * value
        whole = [sums_ref[g, n] for n in range(poles)]
        for u in range(units):
            state = scan_unit(p_ref, fac_ref, None, g, u * tokens, seg, None)
            whole = [span_ref[g, n] * whole[n] + state[n] for n in range(poles)]
        for n in range(poles):
            found = jnp.sum(end_ref[g, n] * whole[n], axis=0, keepdims=True)
            end_state_ref[pl.ds(g * poles + n, 1), :] = found
        return c

    lax.fori_loop(0, groups, body, 0)


def starts_kernel(seg, fac_ref, rin_ref, scan_ref, skip_ref, p_ref, *refs):
    *ends_refs, z_ref, begin_ref, mine_ref = refs
    ends_refs = [ref.at[u] for ref in (*ends_refs, mine_ref) for u in range(ref.shape[0])]
    groups, poles = fac_ref.shape[0], fac_ref.shape[1]
    row = lax.broadcasted_iota(jnp.int32, (SEGS, LANES), 0)

    def body(g, c):
        for u in range(mine_ref.shape[0]):
            state = scan_unit(p_ref, fac_ref, rin_ref, g, u * seg * SEGS, seg, z_ref)
            for n in range(poles):
                mine_ref[u, g, n] = state[n]
        lanes = pl.ds(pl.multiple_of(g * LANES, LANES), LANES)
        z_ref[g] = z_ref[g] + skip_ref[:, lanes] * p_ref[g]

        def pole(n, c):
            lead = rin_ref[g, n] * fac_ref[g, n]
            step = jnp.broadcast_to(scan_ref[0, g, n, 1:2, :], (SEGS, LANES))
            enter = jnp.zeros((SEGS, LANES), F32)
            for k, ends_ref in enumerate(ends_refs):
                held = ends_ref[g, n]
                held = jnp.where(row == 0, held + step * enter, held)
                for b, by in enumerate((1, 2, 4)):
                    held = held + scan_ref[b, g, n] * pltpu.roll(held, by, 0)
                begin_ref[k, g, n] = lead * jnp.where(row == 0, enter, pltpu.roll(held, 1, 0))
                enter = jnp.broadcast_to(held[SEGS - 1 :, :], (SEGS, LANES))
            return c

        lax.fori_loop(0, poles, pole, 0, unroll=4)
        return c

    lax.fori_loop(0, groups, body, 0)


def final_kernel(
    units, seg, hops, pieces, paired, fac_ref, reach_ref, begin_ref, inj_ref, from_cache_ref, jump_ref, *refs
):
    e_refs = refs[:hops]
    q_refs = refs[hops : hops + pieces]
    z_refs = refs[hops + pieces : hops + 2 * pieces]
    out_ref, add_ref, enter_ref = refs[hops + 2 * pieces :]
    groups, poles = fac_ref.shape[0], fac_ref.shape[1]
    tokens = seg * SEGS
    position = lax.axis_index("context")

    for g in range(groups):
        lanes = slice(g * LANES, (g + 1) * LANES)
        rows = slice(g * poles, (g + 1) * poles)
        jump = jump_ref[:, lanes]
        total = jnp.zeros((poles, LANES), F32)
        for e in range(hops):
            found = e_refs[e][rows, :]
            if paired:
                source = position ^ (e + 1)
                gap = position - 1 - source
                for step in range(1, hops):
                    found = jnp.where(gap >= step, found * jump, found)
                found = jnp.where(gap >= 0, found, 0.0)
            total = total + found
        enter_ref[g] = inj_ref[:, lanes] * total + from_cache_ref[:, lanes]

    def body(step, c):
        k, g = step // groups, step % groups
        state = []
        for n in range(poles):
            enter = jnp.broadcast_to(enter_ref[g, n : n + 1, :], (SEGS, LANES))
            state.append(begin_ref[k, g, n] + reach_ref[k, g, n] * enter)
        for j in range(seg):
            if j:
                state = [fac_ref[g, n] * state[n] for n in range(poles)]
            terms = state
            while len(terms) > 1:
                terms = [a + b for a, b in zip(terms[::2], terms[1::2])]
            add_ref[step, pl.ds(j, SEGS, stride=seg), :] = terms[0]
        return c

    lax.fori_loop(0, units * groups, body, 0)
    k = 0
    for q_ref, z_ref in zip(q_refs, z_refs):
        for u in range(q_ref.shape[1] // tokens):
            here = slice(u * tokens, (u + 1) * tokens)
            for g in range(groups):
                out_ref[k * tokens : (k + 1) * tokens, g * LANES : (g + 1) * LANES] = (
                    q_ref[g, here, :] * (z_ref[g, here, :] + add_ref[k * groups + g])
                ).astype(BF16)
            k += 1


def local(
    hidden, norm_gain, in_proj, short_filter, conv_cache, decay, residues, skip_gain, cached_state
):
    count, width = hidden.shape
    chans = in_proj.shape[2]
    poles = decay.shape[1]
    taps = short_filter.shape[0]
    groups = chans // LANES
    units = 8
    tokens = count // units
    seg = tokens // SEGS
    position = lax.axis_index("context").astype(F32)
    contexts = lax.axis_size("context")

    head = [(count - TAIL, TAIL), (0, tokens)]
    sizes = [2 * tokens, 2 * tokens + TAIL, 3 * tokens - 2 * TAIL]
    taken = [3, 2, 3]
    rest, at = [], tokens
    for size in sizes:
        rest.append((at, size))
        at += size
    *own, squares = call(
        functools.partial(open_kernel, [head] + [[part] for part in rest]),
        [kept(tokens + TAIL + NOTES, width, dtype=BF16)]
        + [kept(n, width, dtype=BF16) for _, n in rest]
        + [kept(count, LANES)],
        [pltpu.VMEM((count, width), BF16), pltpu.SemaphoreType.DMA((len(rest) + 3,))],
        (hidden,),
        anywhere=(0,),
    )
    far = [flipped(block, 2) for block in own]
    hidden, own = lax.optimization_barrier((hidden, own))
    sib = flipped(hidden, 1)

    filt = short_filter.transpose(1, 0, 2)
    gain = norm_gain[None]
    skip = skip_gain[None]
    dec, res = decay.T, residues.T
    inj = jnp.sqrt(-jnp.expm1(-2.0 * dec))
    jump = jnp.exp(-dec * count)
    from_cache = jnp.exp(-dec * (count * position)) * cached_state.T
    cache = jnp.pad(conv_cache.astype(F32), ((HALO - taps + 1, 0), (0, 0), (0, 0)))
    cache = cache.reshape(HALO, 3 * groups, LANES).transpose(1, 0, 2)
    tile = (groups, poles, SEGS, LANES)
    w = in_proj.transpose(1, 0, 2)
    w, inj, jump, from_cache, cache = lax.optimization_barrier((w, inj, jump, from_cache, cache))
    w, fac, rin, scan, span, end, reach = call(
        functools.partial(stage_kernel, seg, units),
        [
            kept(*w.shape, dtype=BF16), kept(*tile), kept(*tile),
            kept(3, *tile), kept(*tile), kept(*tile), kept(units, *tile),
        ],
        [pltpu.SemaphoreType.DMA((1,))],
        (w, dec, res, inj),
        anywhere=(0,),
    )

    def streams_of(rows, dtype=F32):
        return sds(3 * groups, rows, LANES, dtype=dtype)

    arrived, fac = lax.optimization_barrier((far[0], fac))
    fwd = flipped(arrived, 1)
    scale, tail, send, body = call(
        functools.partial(head_kernel, head),
        [sds(count, LANES), streams_of(TAIL), streams_of(HALO, BF16), streams_of(tokens)],
        [pltpu.VMEM((TAIL + tokens, D), BF16)],
        (own[0], sib, arrived, fwd, squares, gain, w),
    )
    prior = shifted(send, "context", 1)
    later = sum(sizes)
    part = call(
        functools.partial(near_kernel, rest),
        streams_of(later),
        [pltpu.VMEM((later, 2 * width), BF16)],
        (*own[1:], sib, scale, gain, w),
    )
    other, after = cache, part
    qs, zs, ends = [], [], []
    offset = 0
    for k, ((a, n), some) in enumerate(zip(rest, taken)):
        plane = (groups, some * tokens, LANES)
        arrived, after = lax.optimization_barrier((far[1 + k], after))
        fwd = flipped(arrived, 1)
        args = (arrived, fwd, scale, gain, w, part, filt, fac)
        own_rows = (body.shape[1] + HALO if k == 0 else prior.shape[1]) + n
        normed = pltpu.VMEM((n, 2 * width), BF16)
        if k < len(rest) - 1:
            q, z, e, sums, last = call(
                functools.partial(chunk_kernel, a, n, offset, some, seg, k == 0),
                [sds(*plane), sds(*plane), sds(some, *tile), sds(*tile), streams_of(own_rows - some * tokens)],
                [pltpu.VMEM((3 * groups, own_rows, LANES), F32), normed, pltpu.VMEM(plane, F32)],
                (*args, rin, span, skip, prior, other, body),
            )
            zs.append(z)
            ends.append(e)
            prior, other, after = last, sums, last
        else:
            q, p, end_state = call(
                functools.partial(last_kernel, a, n, offset, some, seg),
                [sds(*plane), sds(*plane), sds(groups * poles, LANES)],
                [pltpu.VMEM((3 * groups, own_rows + TAIL, LANES), F32), normed],
                (*args, span, end, prior, other, tail),
            )
        qs.append(q)
        offset += n
    paired = contexts == 4
    if paired:
        before = [
            lax.ppermute(end_state, "context", [(i, i ^ d) for i in range(contexts)]) for d in range(1, contexts)
        ]
    else:
        every = lax.all_gather(end_state.reshape(groups, poles, LANES), "context")
        gaps = position - 1.0 - jnp.arange(contexts, dtype=F32)
        rates = dec.reshape(poles, groups, LANES).transpose(1, 0, 2)
        weights = jnp.where(
            (gaps >= 0.0)[:, None, None, None],
            jnp.exp(-rates[None] * count * jnp.maximum(gaps, 0.0)[:, None, None, None]),
            0.0,
        )
        before = [jnp.sum(weights * every, axis=0).reshape(groups * poles, LANES)]
    z, begin = call(
        functools.partial(starts_kernel, seg),
        [sds(*plane), sds(units, *tile)],
        [pltpu.VMEM((taken[-1], *tile), F32)],
        (fac, rin, scan, skip, p, *ends),
    )
    zs.append(z)
    return call(
        functools.partial(final_kernel, units, seg, len(before), len(qs), paired),
        sds(count, chans, dtype=BF16),
        [pltpu.VMEM((units * groups, tokens, LANES), F32), pltpu.VMEM((groups, poles, LANES), F32)],
        (fac, reach, begin, inj, from_cache, jump, *before, *qs, *zs),
    )


def solution(mesh):
    placed = (
        P(("groups", "context"), "tensor"),
        P(),
        P(None, None, "tensor"),
        P(None, None, "tensor"),
        P("groups", None, "tensor"),
        P("tensor", None),
        P("tensor", None),
        P("tensor"),
        P(("groups", "tensor"), None),
    )
    return jax.shard_map(
        local,
        mesh=mesh,
        in_specs=placed,
        out_specs=P(("groups", "context"), "tensor"),
        check_vma=False,
    )
```

```python
import functools

import jax
import jax.numpy as jnp
from jax import lax
from jax.experimental import pallas as pl
from jax.experimental.pallas import tpu as pltpu
from jax.sharding import PartitionSpec as P

D = 4096
EPS = 1e-06
LANES = 128
SEGS = 8
TAIL = 16
HALO = 8
NOTES = 8

VM = pl.BlockSpec(memory_space=pltpu.VMEM)
F32 = jnp.float32
BF16 = jnp.bfloat16


def shifted(block, axis, distance):
    size = lax.axis_size(axis)
    return lax.ppermute(block, axis, [(i - distance, i) for i in range(distance, size)])


def paired_with(block, bits):
    size = lax.axis_size("context")
    return lax.ppermute(block, "context", [(i, i ^ bits) for i in range(size)])


def flipped(block, bit):
    size = lax.axis_size("tensor")
    return lax.ppermute(block, "tensor", [(i, i ^ bit) for i in range(size)])


def call(kernel, outs, scratch, args, flops=0, limit=12, anywhere=()):
    specs = [pl.BlockSpec(memory_space=pltpu.HBM) if i in anywhere else VM for i in range(len(args))]
    args = [pltpu.with_memory_space_constraint(x, pltpu.HBM) if i in anywhere else x for i, x in enumerate(args)]
    return pl.pallas_call(
        kernel,
        out_shape=outs,
        in_specs=specs,
        out_specs=jax.tree.map(lambda _: VM, outs, is_leaf=lambda o: hasattr(o, "dtype")),
        scratch_shapes=scratch,
        cost_estimate=pl.CostEstimate(flops=flops, bytes_accessed=1024, transcendentals=0),
        compiler_params=pltpu.CompilerParams(vmem_limit_bytes=limit << 20),
    )(*args)


def kept(*shape, dtype=F32):
    return pltpu.VMEM(shape, dtype)


def sds(*shape, dtype=F32):
    return jax.ShapeDtypeStruct(shape, dtype)


def open_kernel(pieces, h_any, *refs):
    *out_refs, squares_ref, h_ref, sem = refs
    count, width = h_ref.shape
    whole = pltpu.make_async_copy(h_any, h_ref, sem.at[0])
    whole.start()
    copies = []
    for parts, out_ref in zip(pieces, out_refs):
        at = 0
        for start, rows in parts:
            copies.append(
                pltpu.make_async_copy(
                    h_any.at[start : start + rows, :], out_ref.at[at : at + rows, :], sem.at[1 + len(copies)]
                )
            )
            at += rows
    for copy in copies:
        copy.start()
    whole.wait()
    sums = []
    for at in range(0, count, LANES):
        squares = row_squares(h_ref, slice(at, at + LANES))
        squares_ref[at : at + LANES, :] = squares
        sums.append(jnp.sum(jnp.transpose(squares), axis=0, keepdims=True))
    rest = jnp.concatenate(sums, axis=1)
    terms = []
    for _ in range(3):
        term = rest.astype(BF16).astype(F32)
        rest = rest - term
        terms.append(term)
    coded = jnp.concatenate(terms + [jnp.zeros((NOTES - 3, count), F32)], axis=0).astype(BF16)
    for copy in copies:
        copy.wait()
    first = out_refs[0]
    at = first.shape[0] - NOTES
    first[at:, :count] = coded
    first[at:, count:] = jnp.zeros((NOTES, width - count), BF16)


def row_squares(ref, rows):
    block = ref[rows, :].astype(F32)
    block = block * block
    total = block[:, :LANES]
    for lane in range(LANES, block.shape[1], LANES):
        total = total + block[:, lane : lane + LANES]
    return total


def stage_kernel(
    seg, chunks, w_any, dec_any, res_any, cache_any, inj_ref,
    w_ref, fac_ref, rin_ref, scan_ref, span_ref, end_ref, reach_ref, prior_ref,
    dec_ref, res_ref, cache_ref, sem,
):
    weights = pltpu.make_async_copy(w_any, w_ref, sem.at[0])
    small = [
        pltpu.make_async_copy(dec_any, dec_ref, sem.at[1]),
        pltpu.make_async_copy(res_any, res_ref, sem.at[2]),
        pltpu.make_async_copy(cache_any, cache_ref, sem.at[3]),
    ]
    for copy in (*small, weights):
        copy.start()
    for copy in small:
        copy.wait()
    cache = cache_ref[...].astype(F32)
    streams, chans = cache.shape[1:]
    for i in range(streams):
        for g in range(chans // LANES):
            rows = cache[:, i, g * LANES : (g + 1) * LANES]
            rows = jnp.concatenate([jnp.zeros((HALO - rows.shape[0], LANES), F32), rows], axis=0)
            prior_ref[i * (chans // LANES) + g] = rows
    groups, poles = fac_ref.shape[0], fac_ref.shape[1]
    row = lax.broadcasted_iota(jnp.int32, (SEGS, LANES), 0)
    rowf = row.astype(F32)

    def body(g, c):
        lanes = pl.ds(pl.multiple_of(g * LANES, LANES), LANES)
        for n in range(poles):
            dec = jnp.broadcast_to(dec_ref[n : n + 1, lanes], (SEGS, LANES))
            res = jnp.broadcast_to(res_ref[n : n + 1, lanes], (SEGS, LANES))
            inj = jnp.broadcast_to(inj_ref[n : n + 1, lanes], (SEGS, LANES))
            fac_ref[g, n] = jnp.exp(-dec)
            rin_ref[g, n] = res * inj
            for b, step in enumerate((1, 2, 4)):
                scan_ref[b, g, n] = jnp.where(row >= step, jnp.exp(-dec * float(seg * step)), 0.0)
            span_ref[g, n] = jnp.exp(-dec * float(seg * SEGS))
            end_ref[g, n] = jnp.exp(-dec * ((SEGS - 1.0 - rowf) * float(seg)))
            for k in range(chunks):
                reach_ref[k, g, n] = res * jnp.exp(-dec * (1.0 + float(seg) * (float(SEGS * k) + rowf)))
        return c

    lax.fori_loop(0, groups, body, 0)
    weights.wait()


def normed_block(ref, rows, scale_ref, start, gain_ref, index):
    width = ref.shape[1]
    lanes = pl.ds(pl.multiple_of(index * width, width), width)
    count = rows.stop - rows.start
    scale = scale_ref[start : start + count, :]
    scale = jnp.concatenate([scale] * (width // LANES), axis=1)
    return (ref[rows, :].astype(F32) * scale * gain_ref[:, lanes]).astype(BF16)


def put_block(normed_ref, rows, index, block):
    width = block.shape[1]
    normed_ref[rows, pl.ds(pl.multiple_of(index * width, width), width)] = block


def multiply(normed_ref, w_ref, start, put):
    groups = w_ref.shape[2] // LANES
    halves = groups // 2
    depth = normed_ref.shape[1]

    def body(step, c):
        i, half = step // halves, step % halves
        lanes = pl.ds(pl.multiple_of(half * 2 * LANES, 2 * LANES), 2 * LANES)
        rows = pl.ds(start, depth)
        products = jnp.dot(normed_ref[...], w_ref[i, rows, lanes], preferred_element_type=F32)
        put(step * 2, products[:, :LANES])
        put(step * 2 + 1, products[:, LANES:])
        return c

    lax.fori_loop(0, 3 * halves, body, 0)


def rounded(streams):
    return streams.astype(BF16).astype(F32)


def convolve(ext_ref, filt_ref, g, first, tokens, streams=(0, 1, 2)):
    groups = ext_ref.shape[0] // 3
    lanes = pl.ds(pl.multiple_of(g * LANES, LANES), LANES)
    taps = filt_ref.shape[1]
    found = []
    for i in streams:
        total = jnp.zeros((tokens, LANES), F32)
        for k in range(taps):
            rows = pl.ds(first + HALO - taps + 1 + k, tokens)
            total = total + filt_ref[i, k : k + 1, lanes] * ext_ref[i * groups + g, rows, :]
        found.append(total)
    return found


def scan_unit(prod_ref, fac_ref, rin_ref, g, first, seg, out_ref):
    poles = fac_ref.shape[1]
    entry = prod_ref[g, pl.ds(first, SEGS, stride=seg), :]
    state = [entry] * poles
    for j in range(seg):
        rows = pl.ds(first + j, SEGS, stride=seg)
        if j:
            entry = prod_ref[g, rows, :]
            state = [fac_ref[g, n] * state[n] + entry for n in range(poles)]
        if out_ref is not None:
            terms = [rin_ref[g, n] * state[n] for n in range(poles)]
            while len(terms) > 1:
                terms = [a + b for a, b in zip(terms[::2], terms[1::2])]
            out_ref[g, rows, :] = terms[0]
    return state


def head_kernel(
    parts, a_ref, sib_ref, far_ref, fwd_ref, squares_ref, gain_ref, w_ref,
    scale_ref, tail_ref, send_ref, body_ref, normed_ref,
):
    t = lax.axis_index("tensor")
    count = squares_ref.shape[0]
    at = far_ref.shape[0] - NOTES
    notes = jnp.zeros((1, count), F32)
    for ref in (sib_ref, far_ref, fwd_ref):
        coded = ref[at:, :count].astype(F32)
        notes = notes + ((coded[0:1] + coded[1:2]) + coded[2:3])
    for row in range(0, count, LANES):
        rows = slice(row, row + LANES)
        others = jnp.transpose(jnp.broadcast_to(notes[:, rows], (LANES, LANES)))
        mine = jnp.sum(squares_ref[rows, :], axis=1, keepdims=True)
        scale_ref[rows, :] = lax.rsqrt((mine + others) / D + EPS)
    at = 0
    for start, rows in parts:
        here = slice(at, at + rows)
        at += rows
        for bits, ref in enumerate((a_ref, sib_ref, far_ref, fwd_ref)):
            index = t ^ bits
            put_block(normed_ref, here, index, normed_block(ref, here, scale_ref, start, gain_ref, index))

    def put(at, products):
        streams = rounded(products)
        tail_ref[at] = streams[:TAIL]
        send_ref[at] = streams[TAIL - HALO : TAIL].astype(BF16)
        body_ref[at] = streams[TAIL:]

    multiply(normed_ref, w_ref, 0, put)


def near_kernel(parts, *refs):
    own_refs = refs[: len(parts)]
    sib_ref, scale_ref, gain_ref, w_ref, part_ref, normed_ref = refs[len(parts) :]
    t = lax.axis_index("tensor")
    depth = normed_ref.shape[1]
    at = 0
    for own_ref, (start, rows) in zip(own_refs, parts):
        here = slice(at, at + rows)
        at += rows
        own = normed_block(own_ref, slice(0, rows), scale_ref, start, gain_ref, t)
        put_block(normed_ref, here, t & 1, own)
        sib = normed_block(sib_ref, slice(start, start + rows), scale_ref, start, gain_ref, t ^ 1)
        put_block(normed_ref, here, (t & 1) ^ 1, sib)

    def put(at, products):
        part_ref[at] = products

    multiply(normed_ref, w_ref, pl.multiple_of((t >> 1) * depth, depth), put)


def far_part(start, rows, offset, far_ref, fwd_ref, scale_ref, gain_ref, w_ref, part_ref, ext_ref, base, normed_ref):
    t = lax.axis_index("tensor")
    depth = normed_ref.shape[1]
    here = slice(0, rows)
    put_block(normed_ref, here, t & 1, normed_block(far_ref, here, scale_ref, start, gain_ref, t ^ 2))
    put_block(normed_ref, here, (t & 1) ^ 1, normed_block(fwd_ref, here, scale_ref, start, gain_ref, t ^ 3))

    def put(at, products):
        ext_ref[at, base : base + rows, :] = rounded(part_ref[at, offset : offset + rows, :] + products)

    multiply(normed_ref, w_ref, pl.multiple_of(((t >> 1) ^ 1) * depth, depth), put)


def chunk_kernel(
    start, rows, offset, units, seg, first,
    far_ref, fwd_ref, scale_ref, gain_ref, w_ref, part_ref, filt_ref, fac_ref, rin_ref, span_ref, skip_ref,
    other_ref, body_ref, *refs,
):
    *prior_refs, q_ref, z_ref, ends_ref, sum_ref, last_ref, ext_ref, normed_ref, prod_ref = refs
    prior_ref = prior_refs[0]
    groups, poles = fac_ref.shape[0], fac_ref.shape[1]
    tokens = seg * SEGS
    if first:
        position = lax.axis_index("context")
        got = prior_ref[...].astype(F32)
        if len(prior_refs) > 1:
            got = jnp.where((position & 1) == 1, got, prior_refs[1][...].astype(F32))
        ext_ref[:, :HALO, :] = jnp.where(position == 0, other_ref[...], got)
        base = HALO + body_ref.shape[1]
        ext_ref[:, HALO:base, :] = body_ref[...]
    else:
        base = prior_ref.shape[1]
        ext_ref[:, :base, :] = prior_ref[...]
    far_part(start, rows, offset, far_ref, fwd_ref, scale_ref, gain_ref, w_ref, part_ref, ext_ref, base, normed_ref)
    last_ref[...] = ext_ref[:, units * tokens :, :]

    def body(g, c):
        lanes = pl.ds(pl.multiple_of(g * LANES, LANES), LANES)
        query, keyed, value = convolve(ext_ref, filt_ref, g, 0, units * tokens)
        q_ref[g] = query
        prod_ref[g] = keyed * value
        for u in range(units):
            state = scan_unit(prod_ref, fac_ref, rin_ref, g, u * tokens, seg, z_ref)
            for n in range(poles):
                ends_ref[u, g, n] = state[n]
                if u:
                    sum_ref[g, n] = span_ref[g, n] * sum_ref[g, n] + state[n]
                elif first:
                    sum_ref[g, n] = state[n]
                else:
                    sum_ref[g, n] = span_ref[g, n] * other_ref[g, n] + state[n]
        z_ref[g] = z_ref[g] + skip_ref[:, lanes] * prod_ref[g]
        return c

    lax.fori_loop(0, groups, body, 0)


def last_kernel(
    start, rows, offset, units, seg,
    far_ref, fwd_ref, scale_ref, gain_ref, w_ref, part_ref, filt_ref, fac_ref, span_ref, end_ref,
    prior_ref, sums_ref, tail_ref,
    q_ref, p_ref, end_state_ref,
    ext_ref, normed_ref,
):
    groups, poles = fac_ref.shape[0], fac_ref.shape[1]
    tokens = seg * SEGS
    base = prior_ref.shape[1]
    ext_ref[:, :base, :] = prior_ref[...]
    ext_ref[:, base + rows :, :] = tail_ref[...]
    far_part(start, rows, offset, far_ref, fwd_ref, scale_ref, gain_ref, w_ref, part_ref, ext_ref, base, normed_ref)

    def body(g, c):
        query, keyed, value = convolve(ext_ref, filt_ref, g, 0, units * tokens)
        q_ref[g] = query
        p_ref[g] = keyed * value
        whole = [sums_ref[g, n] for n in range(poles)]
        for u in range(units):
            state = scan_unit(p_ref, fac_ref, None, g, u * tokens, seg, None)
            whole = [span_ref[g, n] * whole[n] + state[n] for n in range(poles)]
        for n in range(poles):
            found = jnp.sum(end_ref[g, n] * whole[n], axis=0, keepdims=True)
            end_state_ref[pl.ds(g * poles + n, 1), :] = found
        return c

    lax.fori_loop(0, groups, body, 0)


def starts_kernel(seg, fac_ref, rin_ref, scan_ref, skip_ref, p_ref, *refs):
    *ends_refs, z_ref, begin_ref, mine_ref = refs
    ends_refs = [ref.at[u] for ref in (*ends_refs, mine_ref) for u in range(ref.shape[0])]
    groups, poles = fac_ref.shape[0], fac_ref.shape[1]
    row = lax.broadcasted_iota(jnp.int32, (SEGS, LANES), 0)

    def body(g, c):
        for u in range(mine_ref.shape[0]):
            state = scan_unit(p_ref, fac_ref, rin_ref, g, u * seg * SEGS, seg, z_ref)
            for n in range(poles):
                mine_ref[u, g, n] = state[n]
        lanes = pl.ds(pl.multiple_of(g * LANES, LANES), LANES)
        z_ref[g] = z_ref[g] + skip_ref[:, lanes] * p_ref[g]

        def pole(n, c):
            lead = rin_ref[g, n] * fac_ref[g, n]
            step = jnp.broadcast_to(scan_ref[0, g, n, 1:2, :], (SEGS, LANES))
            enter = jnp.zeros((SEGS, LANES), F32)
            for k, ends_ref in enumerate(ends_refs):
                held = ends_ref[g, n]
                held = jnp.where(row == 0, held + step * enter, held)
                for b, by in enumerate((1, 2, 4)):
                    held = held + scan_ref[b, g, n] * pltpu.roll(held, by, 0)
                begin_ref[k, g, n] = lead * jnp.where(row == 0, enter, pltpu.roll(held, 1, 0))
                enter = jnp.broadcast_to(held[SEGS - 1 :, :], (SEGS, LANES))
            return c

        lax.fori_loop(0, poles, pole, 0, unroll=4)
        return c

    lax.fori_loop(0, groups, body, 0)


def final_kernel(
    units, seg, hops, pieces, paired, fac_ref, reach_ref, begin_ref, inj_ref, from_cache_ref, jump_ref, *refs
):
    e_refs = refs[:hops]
    q_refs = refs[hops : hops + pieces]
    z_refs = refs[hops + pieces : hops + 2 * pieces]
    out_ref, add_ref, enter_ref = refs[hops + 2 * pieces :]
    groups, poles = fac_ref.shape[0], fac_ref.shape[1]
    tokens = seg * SEGS
    position = lax.axis_index("context")

    for g in range(groups):
        lanes = slice(g * LANES, (g + 1) * LANES)
        rows = slice(g * poles, (g + 1) * poles)
        jump = jump_ref[:, lanes]
        total = jnp.zeros((poles, LANES), F32)
        for e in range(hops):
            found = e_refs[e][rows, :]
            if paired:
                source = position ^ (e + 1)
                gap = position - 1 - source
                for step in range(1, hops):
                    found = jnp.where(gap >= step, found * jump, found)
                found = jnp.where(gap >= 0, found, 0.0)
            total = total + found
        enter_ref[g] = inj_ref[:, lanes] * total + from_cache_ref[:, lanes]

    def body(step, c):
        k, g = step // groups, step % groups
        state = []
        for n in range(poles):
            enter = jnp.broadcast_to(enter_ref[g, n : n + 1, :], (SEGS, LANES))
            state.append(begin_ref[k, g, n] + reach_ref[k, g, n] * enter)
        for j in range(seg):
            if j:
                state = [fac_ref[g, n] * state[n] for n in range(poles)]
            terms = state
            while len(terms) > 1:
                terms = [a + b for a, b in zip(terms[::2], terms[1::2])]
            add_ref[step, pl.ds(j, SEGS, stride=seg), :] = terms[0]
        return c

    lax.fori_loop(0, units * groups, body, 0)
    k = 0
    for q_ref, z_ref in zip(q_refs, z_refs):
        for u in range(q_ref.shape[1] // tokens):
            here = slice(u * tokens, (u + 1) * tokens)
            for g in range(groups):
                out_ref[k * tokens : (k + 1) * tokens, g * LANES : (g + 1) * LANES] = (
                    q_ref[g, here, :] * (z_ref[g, here, :] + add_ref[k * groups + g])
                ).astype(BF16)
            k += 1


def local(
    hidden, norm_gain, in_proj, short_filter, conv_cache, decay, residues, skip_gain, cached_state
):
    count, width = hidden.shape
    chans = in_proj.shape[2]
    poles = decay.shape[1]
    taps = short_filter.shape[0]
    groups = chans // LANES
    units = 8
    tokens = count // units
    seg = tokens // SEGS
    position = lax.axis_index("context").astype(F32)
    contexts = lax.axis_size("context")

    head = [(count - TAIL, TAIL), (0, tokens)]
    sizes = [2 * tokens, 2 * tokens + TAIL, 3 * tokens - 2 * TAIL]
    taken = [3, 2, 3]
    rest, at = [], tokens
    for size in sizes:
        rest.append((at, size))
        at += size
    *own, squares = call(
        functools.partial(open_kernel, [head] + [[part] for part in rest]),
        [kept(tokens + TAIL + NOTES, width, dtype=BF16)]
        + [kept(n, width, dtype=BF16) for _, n in rest]
        + [kept(count, LANES)],
        [pltpu.VMEM((count, width), BF16), pltpu.SemaphoreType.DMA((len(rest) + 3,))],
        (hidden,),
        anywhere=(0,),
    )
    far = [flipped(block, 2) for block in own]
    filt = short_filter.transpose(1, 0, 2)
    gain = norm_gain[None]
    skip = skip_gain[None]
    dec, res = decay.T, residues.T
    inj = jnp.sqrt(-jnp.expm1(-2.0 * dec))
    jump = jnp.exp(-dec * count)
    from_cache = jnp.exp(-dec * (count * position)) * cached_state.T
    tile = (groups, poles, SEGS, LANES)
    w = in_proj.transpose(1, 0, 2)
    w, inj, jump, from_cache = lax.optimization_barrier((w, inj, jump, from_cache))
    w, fac, rin, scan, span, end, reach, cache = call(
        functools.partial(stage_kernel, seg, units),
        [
            kept(*w.shape, dtype=BF16), kept(*tile), kept(*tile),
            kept(3, *tile), kept(*tile), kept(*tile), kept(units, *tile), kept(3 * groups, HALO, LANES),
        ],
        [
            pltpu.VMEM(dec.shape, F32), pltpu.VMEM(res.shape, F32), pltpu.VMEM(conv_cache.shape, BF16),
            pltpu.SemaphoreType.DMA((4,)),
        ],
        (w, dec, res, conv_cache, inj),
        anywhere=(0, 1, 2, 3),
    )

    def streams_of(rows, dtype=F32):
        return sds(3 * groups, rows, LANES, dtype=dtype)

    arrived, mine, hidden, fac = lax.optimization_barrier((far[0], own[0], hidden, fac))
    fwd, sib_first = flipped(arrived, 1), flipped(mine, 1)
    sib = flipped(hidden, 1)
    scale, tail, send, body = call(
        functools.partial(head_kernel, head),
        [sds(count, LANES), streams_of(TAIL), streams_of(HALO, BF16), streams_of(tokens)],
        [pltpu.VMEM((TAIL + tokens, D), BF16)],
        (own[0], sib_first, arrived, fwd, squares, gain, w),
    )
    if contexts == 4:
        prior = paired_with(send, 1), paired_with(send, 3)
    else:
        prior = (shifted(send, "context", 1),)
    later = sum(sizes)
    part = call(
        functools.partial(near_kernel, rest),
        streams_of(later),
        [pltpu.VMEM((later, 2 * width), BF16)],
        (*own[1:], sib, scale, gain, w),
    )
    other, after = cache, part
    qs, zs, ends = [], [], []
    offset = 0
    for k, ((a, n), some) in enumerate(zip(rest, taken)):
        plane = (groups, some * tokens, LANES)
        arrived, after = lax.optimization_barrier((far[1 + k], after))
        fwd = after = flipped(arrived, 1)
        args = (arrived, fwd, scale, gain, w, part, filt, fac)
        own_rows = (body.shape[1] + HALO if k == 0 else prior[0].shape[1]) + n
        normed = pltpu.VMEM((n, 2 * width), BF16)
        if k < len(rest) - 1:
            q, z, e, sums, last = call(
                functools.partial(chunk_kernel, a, n, offset, some, seg, k == 0),
                [sds(*plane), sds(*plane), sds(some, *tile), sds(*tile), streams_of(own_rows - some * tokens)],
                [pltpu.VMEM((3 * groups, own_rows, LANES), F32), normed, pltpu.VMEM(plane, F32)],
                (*args, rin, span, skip, other, body, *prior),
            )
            zs.append(z)
            ends.append(e)
            prior, other, after = (last,), sums, last if k else after
        else:
            q, p, end_state = call(
                functools.partial(last_kernel, a, n, offset, some, seg),
                [sds(*plane), sds(*plane), sds(groups * poles, LANES)],
                [pltpu.VMEM((3 * groups, own_rows + TAIL, LANES), F32), normed],
                (*args, span, end, *prior, other, tail),
            )
        qs.append(q)
        offset += n
    paired = contexts == 4
    if paired:
        before = [paired_with(end_state, d) for d in range(1, contexts)]
    else:
        every = lax.all_gather(end_state.reshape(groups, poles, LANES), "context")
        gaps = position - 1.0 - jnp.arange(contexts, dtype=F32)
        rates = dec.reshape(poles, groups, LANES).transpose(1, 0, 2)
        weights = jnp.where(
            (gaps >= 0.0)[:, None, None, None],
            jnp.exp(-rates[None] * count * jnp.maximum(gaps, 0.0)[:, None, None, None]),
            0.0,
        )
        before = [jnp.sum(weights * every, axis=0).reshape(groups * poles, LANES)]
    z, begin = call(
        functools.partial(starts_kernel, seg),
        [sds(*plane), sds(units, *tile)],
        [pltpu.VMEM((taken[-1], *tile), F32)],
        (fac, rin, scan, skip, p, *ends),
    )
    zs.append(z)
    return call(
        functools.partial(final_kernel, units, seg, len(before), len(qs), paired),
        sds(count, chans, dtype=BF16),
        [pltpu.VMEM((units * groups, tokens, LANES), F32), pltpu.VMEM((groups, poles, LANES), F32)],
        (fac, reach, begin, inj, from_cache, jump, *before, *qs, *zs),
    )


def solution(mesh):
    placed = (
        P(("groups", "context"), "tensor"),
        P(),
        P(None, None, "tensor"),
        P(None, None, "tensor"),
        P("groups", None, "tensor"),
        P("tensor", None),
        P("tensor", None),
        P("tensor"),
        P(("groups", "tensor"), None),
    )
    return jax.shard_map(
        local,
        mesh=mesh,
        in_specs=placed,
        out_specs=P(("groups", "context"), "tensor"),
        check_vma=False,
    )
```

```python
import functools

import jax
import jax.numpy as jnp
from jax import lax
from jax.experimental import pallas as pl
from jax.experimental.pallas import tpu as pltpu
from jax.sharding import PartitionSpec as P

D = 4096
EPS = 1e-06
LANES = 128
SEGS = 8
TAIL = 16
HALO = 8
NOTES = 8

VM = pl.BlockSpec(memory_space=pltpu.VMEM)
F32 = jnp.float32
BF16 = jnp.bfloat16


def shifted(block, axis, distance):
    size = lax.axis_size(axis)
    return lax.ppermute(block, axis, [(i - distance, i) for i in range(distance, size)])


def paired_with(block, bits):
    size = lax.axis_size("context")
    return lax.ppermute(block, "context", [(i, i ^ bits) for i in range(size)])


def flipped(block, bit):
    size = lax.axis_size("tensor")
    return lax.ppermute(block, "tensor", [(i, i ^ bit) for i in range(size)])


def call(kernel, outs, scratch, args, flops=0, limit=12, anywhere=()):
    specs = [pl.BlockSpec(memory_space=pltpu.HBM) if i in anywhere else VM for i in range(len(args))]
    args = [pltpu.with_memory_space_constraint(x, pltpu.HBM) if i in anywhere else x for i, x in enumerate(args)]
    return pl.pallas_call(
        kernel,
        out_shape=outs,
        in_specs=specs,
        out_specs=jax.tree.map(lambda _: VM, outs, is_leaf=lambda o: hasattr(o, "dtype")),
        scratch_shapes=scratch,
        cost_estimate=pl.CostEstimate(flops=flops, bytes_accessed=1024, transcendentals=0),
        compiler_params=pltpu.CompilerParams(vmem_limit_bytes=limit << 20),
    )(*args)


def kept(*shape, dtype=F32):
    return pltpu.VMEM(shape, dtype)


def sds(*shape, dtype=F32):
    return jax.ShapeDtypeStruct(shape, dtype)


def open_kernel(pieces, h_any, *refs):
    *out_refs, squares_ref, h_ref, sem = refs
    count, width = h_ref.shape
    whole = pltpu.make_async_copy(h_any, h_ref, sem.at[0])
    whole.start()
    copies = []
    for parts, out_ref in zip(pieces, out_refs):
        at = 0
        for start, rows in parts:
            copies.append(
                pltpu.make_async_copy(
                    h_any.at[start : start + rows, :], out_ref.at[at : at + rows, :], sem.at[1 + len(copies)]
                )
            )
            at += rows
    for copy in copies:
        copy.start()
    whole.wait()
    sums = []
    for at in range(0, count, LANES):
        squares = row_squares(h_ref, slice(at, at + LANES))
        squares_ref[at : at + LANES, :] = squares
        sums.append(jnp.sum(jnp.transpose(squares), axis=0, keepdims=True))
    rest = jnp.concatenate(sums, axis=1)
    terms = []
    for _ in range(3):
        term = rest.astype(BF16).astype(F32)
        rest = rest - term
        terms.append(term)
    coded = jnp.concatenate(terms + [jnp.zeros((NOTES - 3, count), F32)], axis=0).astype(BF16)
    for copy in copies:
        copy.wait()
    first = out_refs[0]
    at = first.shape[0] - NOTES
    first[at:, :count] = coded
    first[at:, count:] = jnp.zeros((NOTES, width - count), BF16)


def row_squares(ref, rows):
    block = ref[rows, :].astype(F32)
    block = block * block
    total = block[:, :LANES]
    for lane in range(LANES, block.shape[1], LANES):
        total = total + block[:, lane : lane + LANES]
    return total


def stage_kernel(
    seg, chunks, w_any, dec_any, res_any, cache_any, inj_ref,
    w_ref, fac_ref, rin_ref, scan_ref, span_ref, end_ref, reach_ref, prior_ref,
    dec_ref, res_ref, cache_ref, sem,
):
    weights = pltpu.make_async_copy(w_any, w_ref, sem.at[0])
    small = [
        pltpu.make_async_copy(dec_any, dec_ref, sem.at[1]),
        pltpu.make_async_copy(res_any, res_ref, sem.at[2]),
        pltpu.make_async_copy(cache_any, cache_ref, sem.at[3]),
    ]
    for copy in (*small, weights):
        copy.start()
    for copy in small:
        copy.wait()
    cache = cache_ref[...].astype(F32)
    streams, chans = cache.shape[1:]
    for i in range(streams):
        for g in range(chans // LANES):
            rows = cache[:, i, g * LANES : (g + 1) * LANES]
            rows = jnp.concatenate([jnp.zeros((HALO - rows.shape[0], LANES), F32), rows], axis=0)
            prior_ref[i * (chans // LANES) + g] = rows
    groups, poles = fac_ref.shape[0], fac_ref.shape[1]
    row = lax.broadcasted_iota(jnp.int32, (SEGS, LANES), 0)
    rowf = row.astype(F32)

    def body(g, c):
        lanes = pl.ds(pl.multiple_of(g * LANES, LANES), LANES)
        for n in range(poles):
            dec = jnp.broadcast_to(dec_ref[n : n + 1, lanes], (SEGS, LANES))
            res = jnp.broadcast_to(res_ref[n : n + 1, lanes], (SEGS, LANES))
            inj = jnp.broadcast_to(inj_ref[n : n + 1, lanes], (SEGS, LANES))
            fac_ref[g, n] = jnp.exp(-dec)
            rin_ref[g, n] = res * inj
            for b, step in enumerate((1, 2, 4)):
                scan_ref[b, g, n] = jnp.where(row >= step, jnp.exp(-dec * float(seg * step)), 0.0)
            span_ref[g, n] = jnp.exp(-dec * float(seg * SEGS))
            end_ref[g, n] = jnp.exp(-dec * ((SEGS - 1.0 - rowf) * float(seg)))
            for k in range(chunks):
                reach_ref[k, g, n] = res * jnp.exp(-dec * (1.0 + float(seg) * (float(SEGS * k) + rowf)))
        return c

    lax.fori_loop(0, groups, body, 0)
    weights.wait()


def normed_block(ref, rows, scale_ref, start, gain_ref, index):
    width = ref.shape[1]
    lanes = pl.ds(pl.multiple_of(index * width, width), width)
    count = rows.stop - rows.start
    scale = scale_ref[start : start + count, :]
    scale = jnp.concatenate([scale] * (width // LANES), axis=1)
    return (ref[rows, :].astype(F32) * scale * gain_ref[:, lanes]).astype(BF16)


def put_block(normed_ref, rows, index, block):
    width = block.shape[1]
    normed_ref[rows, pl.ds(pl.multiple_of(index * width, width), width)] = block


def multiply(normed_ref, w_ref, start, put):
    groups = w_ref.shape[2] // LANES
    halves = groups // 2
    depth = normed_ref.shape[1]

    def body(step, c):
        i, half = step // halves, step % halves
        lanes = pl.ds(pl.multiple_of(half * 2 * LANES, 2 * LANES), 2 * LANES)
        rows = pl.ds(start, depth)
        products = jnp.dot(normed_ref[...], w_ref[i, rows, lanes], preferred_element_type=F32)
        put(step * 2, products[:, :LANES])
        put(step * 2 + 1, products[:, LANES:])
        return c

    lax.fori_loop(0, 3 * halves, body, 0)


def rounded(streams):
    return streams.astype(BF16).astype(F32)


def convolve(ext_ref, filt_ref, g, first, tokens, streams=(0, 1, 2)):
    groups = ext_ref.shape[0] // 3
    lanes = pl.ds(pl.multiple_of(g * LANES, LANES), LANES)
    taps = filt_ref.shape[1]
    found = []
    for i in streams:
        total = jnp.zeros((tokens, LANES), F32)
        for k in range(taps):
            rows = pl.ds(first + HALO - taps + 1 + k, tokens)
            total = total + filt_ref[i, k : k + 1, lanes] * ext_ref[i * groups + g, rows, :]
        found.append(total)
    return found


def scan_unit(prod_ref, fac_ref, rin_ref, g, first, seg, out_ref):
    poles = fac_ref.shape[1]
    entry = prod_ref[g, pl.ds(first, SEGS, stride=seg), :]
    state = [entry] * poles
    for j in range(seg):
        rows = pl.ds(first + j, SEGS, stride=seg)
        if j:
            entry = prod_ref[g, rows, :]
            state = [fac_ref[g, n] * state[n] + entry for n in range(poles)]
        if out_ref is not None:
            terms = [rin_ref[g, n] * state[n] for n in range(poles)]
            while len(terms) > 1:
                terms = [a + b for a, b in zip(terms[::2], terms[1::2])]
            out_ref[g, rows, :] = terms[0]
    return state


def head_kernel(
    parts, a_ref, sib_ref, far_ref, fwd_ref, squares_ref, gain_ref, w_ref,
    scale_ref, tail_ref, send_ref, body_ref, normed_ref,
):
    t = lax.axis_index("tensor")
    count = squares_ref.shape[0]
    at = far_ref.shape[0] - NOTES
    notes = jnp.zeros((1, count), F32)
    for ref in (far_ref, fwd_ref):
        coded = ref[at:, :count].astype(F32)
        notes = notes + ((coded[0:1] + coded[1:2]) + coded[2:3])
    for row in range(0, count, LANES):
        rows = slice(row, row + LANES)
        others = jnp.transpose(jnp.broadcast_to(notes[:, rows], (LANES, LANES)))
        near = jnp.sum(squares_ref[rows, :] + row_squares(sib_ref, rows), axis=1, keepdims=True)
        scale_ref[rows, :] = lax.rsqrt((near + others) / D + EPS)
    at = 0
    for start, rows in parts:
        here = slice(at, at + rows)
        there = slice(start, start + rows)
        at += rows
        for bits, (ref, where) in enumerate(((a_ref, here), (sib_ref, there), (far_ref, here), (fwd_ref, here))):
            index = t ^ bits
            put_block(normed_ref, here, index, normed_block(ref, where, scale_ref, start, gain_ref, index))

    def put(at, products):
        streams = rounded(products)
        tail_ref[at] = streams[:TAIL]
        send_ref[at] = streams[TAIL - HALO : TAIL].astype(BF16)
        body_ref[at] = streams[TAIL:]

    multiply(normed_ref, w_ref, 0, put)


def near_kernel(parts, *refs):
    own_refs = refs[: len(parts)]
    sib_ref, scale_ref, gain_ref, w_ref, part_ref, normed_ref = refs[len(parts) :]
    t = lax.axis_index("tensor")
    depth = normed_ref.shape[1]
    at = 0
    for own_ref, (start, rows) in zip(own_refs, parts):
        here = slice(at, at + rows)
        at += rows
        own = normed_block(own_ref, slice(0, rows), scale_ref, start, gain_ref, t)
        put_block(normed_ref, here, t & 1, own)
        sib = normed_block(sib_ref, slice(start, start + rows), scale_ref, start, gain_ref, t ^ 1)
        put_block(normed_ref, here, (t & 1) ^ 1, sib)

    def put(at, products):
        part_ref[at] = products

    multiply(normed_ref, w_ref, pl.multiple_of((t >> 1) * depth, depth), put)


def far_part(start, rows, offset, far_ref, fwd_ref, scale_ref, gain_ref, w_ref, part_ref, ext_ref, base, normed_ref):
    t = lax.axis_index("tensor")
    depth = normed_ref.shape[1]
    here = slice(0, rows)
    put_block(normed_ref, here, t & 1, normed_block(far_ref, here, scale_ref, start, gain_ref, t ^ 2))
    put_block(normed_ref, here, (t & 1) ^ 1, normed_block(fwd_ref, here, scale_ref, start, gain_ref, t ^ 3))

    def put(at, products):
        ext_ref[at, base : base + rows, :] = rounded(part_ref[at, offset : offset + rows, :] + products)

    multiply(normed_ref, w_ref, pl.multiple_of(((t >> 1) ^ 1) * depth, depth), put)


def chunk_kernel(
    start, rows, offset, units, seg, first,
    far_ref, fwd_ref, scale_ref, gain_ref, w_ref, part_ref, filt_ref, fac_ref, rin_ref, span_ref, skip_ref,
    other_ref, body_ref, *refs,
):
    *prior_refs, q_ref, z_ref, ends_ref, sum_ref, last_ref, ext_ref, normed_ref, prod_ref = refs
    prior_ref = prior_refs[0]
    groups, poles = fac_ref.shape[0], fac_ref.shape[1]
    tokens = seg * SEGS
    if first:
        position = lax.axis_index("context")
        got = prior_ref[...].astype(F32)
        if len(prior_refs) > 1:
            got = jnp.where((position & 1) == 1, got, prior_refs[1][...].astype(F32))
        ext_ref[:, :HALO, :] = jnp.where(position == 0, other_ref[...], got)
        base = HALO + body_ref.shape[1]
        ext_ref[:, HALO:base, :] = body_ref[...]
    else:
        base = prior_ref.shape[1]
        ext_ref[:, :base, :] = prior_ref[...]
    far_part(start, rows, offset, far_ref, fwd_ref, scale_ref, gain_ref, w_ref, part_ref, ext_ref, base, normed_ref)
    last_ref[...] = ext_ref[:, units * tokens :, :]

    def body(g, c):
        lanes = pl.ds(pl.multiple_of(g * LANES, LANES), LANES)
        query, keyed, value = convolve(ext_ref, filt_ref, g, 0, units * tokens)
        q_ref[g] = query
        prod_ref[g] = keyed * value
        for u in range(units):
            state = scan_unit(prod_ref, fac_ref, rin_ref, g, u * tokens, seg, z_ref)
            for n in range(poles):
                ends_ref[u, g, n] = state[n]
                if u:
                    sum_ref[g, n] = span_ref[g, n] * sum_ref[g, n] + state[n]
                elif first:
                    sum_ref[g, n] = state[n]
                else:
                    sum_ref[g, n] = span_ref[g, n] * other_ref[g, n] + state[n]
        z_ref[g] = z_ref[g] + skip_ref[:, lanes] * prod_ref[g]
        return c

    lax.fori_loop(0, groups, body, 0)


def last_kernel(
    start, rows, offset, units, seg,
    far_ref, fwd_ref, scale_ref, gain_ref, w_ref, part_ref, filt_ref, fac_ref, span_ref, end_ref,
    prior_ref, sums_ref, tail_ref,
    q_ref, p_ref, end_state_ref,
    ext_ref, normed_ref,
):
    groups, poles = fac_ref.shape[0], fac_ref.shape[1]
    tokens = seg * SEGS
    base = prior_ref.shape[1]
    ext_ref[:, :base, :] = prior_ref[...]
    ext_ref[:, base + rows :, :] = tail_ref[...]
    far_part(start, rows, offset, far_ref, fwd_ref, scale_ref, gain_ref, w_ref, part_ref, ext_ref, base, normed_ref)

    def body(g, c):
        query, keyed, value = convolve(ext_ref, filt_ref, g, 0, units * tokens)
        q_ref[g] = query
        p_ref[g] = keyed * value
        whole = [sums_ref[g, n] for n in range(poles)]
        for u in range(units):
            state = scan_unit(p_ref, fac_ref, None, g, u * tokens, seg, None)
            whole = [span_ref[g, n] * whole[n] + state[n] for n in range(poles)]
        for n in range(poles):
            found = jnp.sum(end_ref[g, n] * whole[n], axis=0, keepdims=True)
            end_state_ref[pl.ds(g * poles + n, 1), :] = found
        return c

    lax.fori_loop(0, groups, body, 0)


def starts_kernel(seg, fac_ref, rin_ref, scan_ref, skip_ref, p_ref, *refs):
    *ends_refs, z_ref, begin_ref, mine_ref = refs
    ends_refs = [ref.at[u] for ref in (*ends_refs, mine_ref) for u in range(ref.shape[0])]
    groups, poles = fac_ref.shape[0], fac_ref.shape[1]
    row = lax.broadcasted_iota(jnp.int32, (SEGS, LANES), 0)

    def body(g, c):
        for u in range(mine_ref.shape[0]):
            state = scan_unit(p_ref, fac_ref, rin_ref, g, u * seg * SEGS, seg, z_ref)
            for n in range(poles):
                mine_ref[u, g, n] = state[n]
        lanes = pl.ds(pl.multiple_of(g * LANES, LANES), LANES)
        z_ref[g] = z_ref[g] + skip_ref[:, lanes] * p_ref[g]

        def pole(n, c):
            lead = rin_ref[g, n] * fac_ref[g, n]
            step = jnp.broadcast_to(scan_ref[0, g, n, 1:2, :], (SEGS, LANES))
            enter = jnp.zeros((SEGS, LANES), F32)
            for k, ends_ref in enumerate(ends_refs):
                held = ends_ref[g, n]
                held = jnp.where(row == 0, held + step * enter, held)
                for b, by in enumerate((1, 2, 4)):
                    held = held + scan_ref[b, g, n] * pltpu.roll(held, by, 0)
                begin_ref[k, g, n] = lead * jnp.where(row == 0, enter, pltpu.roll(held, 1, 0))
                enter = jnp.broadcast_to(held[SEGS - 1 :, :], (SEGS, LANES))
            return c

        lax.fori_loop(0, poles, pole, 0, unroll=4)
        return c

    lax.fori_loop(0, groups, body, 0)


def final_kernel(
    units, seg, hops, pieces, paired, fac_ref, reach_ref, begin_ref, inj_ref, from_cache_ref, jump_ref, *refs
):
    e_refs = refs[:hops]
    q_refs = refs[hops : hops + pieces]
    z_refs = refs[hops + pieces : hops + 2 * pieces]
    out_ref, add_ref, enter_ref = refs[hops + 2 * pieces :]
    groups, poles = fac_ref.shape[0], fac_ref.shape[1]
    tokens = seg * SEGS
    position = lax.axis_index("context")

    for g in range(groups):
        lanes = slice(g * LANES, (g + 1) * LANES)
        rows = slice(g * poles, (g + 1) * poles)
        jump = jump_ref[:, lanes]
        total = jnp.zeros((poles, LANES), F32)
        for e in range(hops):
            found = e_refs[e][rows, :]
            if paired:
                source = position ^ (e + 1)
                gap = position - 1 - source
                for step in range(1, hops):
                    found = jnp.where(gap >= step, found * jump, found)
                found = jnp.where(gap >= 0, found, 0.0)
            total = total + found
        enter_ref[g] = inj_ref[:, lanes] * total + from_cache_ref[:, lanes]

    def body(step, c):
        k, g = step // groups, step % groups
        state = []
        for n in range(poles):
            enter = jnp.broadcast_to(enter_ref[g, n : n + 1, :], (SEGS, LANES))
            state.append(begin_ref[k, g, n] + reach_ref[k, g, n] * enter)
        for j in range(seg):
            if j:
                state = [fac_ref[g, n] * state[n] for n in range(poles)]
            terms = state
            while len(terms) > 1:
                terms = [a + b for a, b in zip(terms[::2], terms[1::2])]
            add_ref[step, pl.ds(j, SEGS, stride=seg), :] = terms[0]
        return c

    lax.fori_loop(0, units * groups, body, 0)
    k = 0
    for q_ref, z_ref in zip(q_refs, z_refs):
        for u in range(q_ref.shape[1] // tokens):
            here = slice(u * tokens, (u + 1) * tokens)
            for g in range(groups):
                out_ref[k * tokens : (k + 1) * tokens, g * LANES : (g + 1) * LANES] = (
                    q_ref[g, here, :] * (z_ref[g, here, :] + add_ref[k * groups + g])
                ).astype(BF16)
            k += 1


def local(
    hidden, norm_gain, in_proj, short_filter, conv_cache, decay, residues, skip_gain, cached_state
):
    count, width = hidden.shape
    chans = in_proj.shape[2]
    poles = decay.shape[1]
    taps = short_filter.shape[0]
    groups = chans // LANES
    units = 8
    tokens = count // units
    seg = tokens // SEGS
    position = lax.axis_index("context").astype(F32)
    contexts = lax.axis_size("context")

    head = [(count - TAIL, TAIL), (0, tokens)]
    sizes = [2 * tokens, 2 * tokens + TAIL, 3 * tokens - 2 * TAIL]
    taken = [3, 2, 3]
    rest, at = [], tokens
    for size in sizes:
        rest.append((at, size))
        at += size
    *own, squares = call(
        functools.partial(open_kernel, [head] + [[part] for part in rest]),
        [kept(tokens + TAIL + NOTES, width, dtype=BF16)]
        + [kept(n, width, dtype=BF16) for _, n in rest]
        + [kept(count, LANES)],
        [pltpu.VMEM((count, width), BF16), pltpu.SemaphoreType.DMA((len(rest) + 3,))],
        (hidden,),
        anywhere=(0,),
    )
    far = [flipped(block, 2) for block in own]
    hidden, own = lax.optimization_barrier((hidden, own))
    sib = flipped(hidden, 1)
    filt = short_filter.transpose(1, 0, 2)
    gain = norm_gain[None]
    skip = skip_gain[None]
    dec, res = decay.T, residues.T
    inj = jnp.sqrt(-jnp.expm1(-2.0 * dec))
    jump = jnp.exp(-dec * count)
    from_cache = jnp.exp(-dec * (count * position)) * cached_state.T
    tile = (groups, poles, SEGS, LANES)
    w = in_proj.transpose(1, 0, 2)
    w, inj, jump, from_cache, own = lax.optimization_barrier((w, inj, jump, from_cache, own))
    w, fac, rin, scan, span, end, reach, cache = call(
        functools.partial(stage_kernel, seg, units),
        [
            kept(*w.shape, dtype=BF16), kept(*tile), kept(*tile),
            kept(3, *tile), kept(*tile), kept(*tile), kept(units, *tile), kept(3 * groups, HALO, LANES),
        ],
        [
            pltpu.VMEM(dec.shape, F32), pltpu.VMEM(res.shape, F32), pltpu.VMEM(conv_cache.shape, BF16),
            pltpu.SemaphoreType.DMA((4,)),
        ],
        (w, dec, res, conv_cache, inj),
        anywhere=(0, 1, 2, 3),
    )

    def streams_of(rows, dtype=F32):
        return sds(3 * groups, rows, LANES, dtype=dtype)

    arrived, fac = lax.optimization_barrier((far[0], fac))
    fwd = flipped(arrived, 1)
    scale, tail, send, body = call(
        functools.partial(head_kernel, head),
        [sds(count, LANES), streams_of(TAIL), streams_of(HALO, BF16), streams_of(tokens)],
        [pltpu.VMEM((TAIL + tokens, D), BF16)],
        (own[0], sib, arrived, fwd, squares, gain, w),
    )
    if contexts == 4:
        prior = paired_with(send, 1), paired_with(send, 3)
    else:
        prior = (shifted(send, "context", 1),)
    later = sum(sizes)
    part = call(
        functools.partial(near_kernel, rest),
        streams_of(later),
        [pltpu.VMEM((later, 2 * width), BF16)],
        (*own[1:], sib, scale, gain, w),
    )
    other, after = cache, (part, *prior)
    qs, zs, ends = [], [], []
    offset = 0
    for k, ((a, n), some) in enumerate(zip(rest, taken)):
        plane = (groups, some * tokens, LANES)
        arrived, after = lax.optimization_barrier((far[1 + k], after))
        if k == 0:
            prior = after[1:]
        fwd = after = flipped(arrived, 1)
        args = (arrived, fwd, scale, gain, w, part, filt, fac)
        own_rows = (body.shape[1] + HALO if k == 0 else prior[0].shape[1]) + n
        normed = pltpu.VMEM((n, 2 * width), BF16)
        if k < len(rest) - 1:
            q, z, e, sums, last = call(
                functools.partial(chunk_kernel, a, n, offset, some, seg, k == 0),
                [sds(*plane), sds(*plane), sds(some, *tile), sds(*tile), streams_of(own_rows - some * tokens)],
                [pltpu.VMEM((3 * groups, own_rows, LANES), F32), normed, pltpu.VMEM(plane, F32)],
                (*args, rin, span, skip, other, body, *prior),
            )
            zs.append(z)
            ends.append(e)
            prior, other, after = (last,), sums, last if k else after
        else:
            q, p, end_state = call(
                functools.partial(last_kernel, a, n, offset, some, seg),
                [sds(*plane), sds(*plane), sds(groups * poles, LANES)],
                [pltpu.VMEM((3 * groups, own_rows + TAIL, LANES), F32), normed],
                (*args, span, end, *prior, other, tail),
            )
        qs.append(q)
        offset += n
    paired = contexts == 4
    if paired:
        before = [paired_with(end_state, d) for d in range(1, contexts)]
    else:
        every = lax.all_gather(end_state.reshape(groups, poles, LANES), "context")
        gaps = position - 1.0 - jnp.arange(contexts, dtype=F32)
        rates = dec.reshape(poles, groups, LANES).transpose(1, 0, 2)
        weights = jnp.where(
            (gaps >= 0.0)[:, None, None, None],
            jnp.exp(-rates[None] * count * jnp.maximum(gaps, 0.0)[:, None, None, None]),
            0.0,
        )
        before = [jnp.sum(weights * every, axis=0).reshape(groups * poles, LANES)]
    z, begin = call(
        functools.partial(starts_kernel, seg),
        [sds(*plane), sds(units, *tile)],
        [pltpu.VMEM((taken[-1], *tile), F32)],
        (fac, rin, scan, skip, p, *ends),
    )
    zs.append(z)
    return call(
        functools.partial(final_kernel, units, seg, len(before), len(qs), paired),
        sds(count, chans, dtype=BF16),
        [pltpu.VMEM((units * groups, tokens, LANES), F32), pltpu.VMEM((groups, poles, LANES), F32)],
        (fac, reach, begin, inj, from_cache, jump, *before, *qs, *zs),
    )


def solution(mesh):
    placed = (
        P(("groups", "context"), "tensor"),
        P(),
        P(None, None, "tensor"),
        P(None, None, "tensor"),
        P("groups", None, "tensor"),
        P("tensor", None),
        P("tensor", None),
        P("tensor"),
        P(("groups", "tensor"), None),
    )
    return jax.shard_map(
        local,
        mesh=mesh,
        in_specs=placed,
        out_specs=P(("groups", "context"), "tensor"),
        check_vma=False,
    )
```
